32 devices in a mesh: grp: 4 (over x, core), rep: 8 (over z, y).
Axes of the slice: x: 2, y: 2, z: 4, core: 2. Of those that a mesh axis runs over, the one named last changes fastest.
Arguments:
- block_input: bfloat16 [8, 512, 960], P('rep', 'grp'), may hold values from -32 to 32
- cotangent: bfloat16 [8, 512, 960], P('rep', 'grp'), may hold values from -6 to 6
- norm_gains: bfloat16 [2, 960], P(None, 'grp'), may hold values from 0.099609375 to 1.8984375
- w_query: bfloat16 [960, 960], P(None, 'grp'), may hold values from -8 to 8
- key_weight: bfloat16 [960, 320], P(None, 'grp'), may hold values from -0.1875 to 0.1875
- value_weight: bfloat16 [960, 320], P(None, 'grp'), may hold values from -0.1875 to 0.1875
- w_out: bfloat16 [960, 960], P(None, 'grp'), may hold values from -0.75 to 0.75
- w_gate: bfloat16 [960, 2560], P(None, 'grp'), may hold values from -0.1875 to 0.1875
- w_up: bfloat16 [960, 2560], P(None, 'grp'), may hold values from -0.1875 to 0.1875
- w_down: bfloat16 [2560, 960], P(None, 'grp'), may hold values from -0.25 to 0.25
Outputs:
- block_output: float32 [8, 512, 960], P('rep', 'grp')
- input_grad: float32 [8, 512, 960], P('rep', 'grp')
- grad_gains: float32 [2, 960], P(None, 'grp')
- grad_query: float32 [960, 960], P('rep', 'grp')
- grad_key: float32 [960, 320], P('rep', 'grp')
- grad_value: float32 [960, 320], P('rep', 'grp')
- grad_out: float32 [960, 960], P('rep', 'grp')
- grad_gate: float32 [960, 2560], P('rep', 'grp')
- grad_up: float32 [960, 2560], P('rep', 'grp')
- grad_down: float32 [2560, 960], P('rep', 'grp')
The draws below stay inside these ranges and needn't reach their ends.
All inputs are finite; a program needn't handle non-finite values.
Results may differ from the reference program's by a relative error of at most 0.014.
Values may be sent and summed in bfloat16 or wider, within the bound.
No kernel may reach another device: no remote copies, remote signals or barrier semaphores. Data moves between devices by JAX's collectives and lax.ppermute only.
A program may use at most 192 MiB of HBM per device.

```python
import math
import jax
import jax.numpy as jnp
from jax import lax

MODEL_WIDTH = 960
HEAD_SIZE = 64
QUERY_HEADS = 15
KEY_VALUE_HEADS = 5
HIDDEN_UNITS = 2560
SEQ_LEN = 512
SEQS = 8


def draw_block_input(key, part):
    base_key = jax.random.fold_in(key, 11)
    first, second, third = jax.random.split(base_key, 3)
    row_scale = jnp.exp(jax.random.uniform(second, (SEQS, SEQ_LEN, 1), jnp.float32, jnp.log(0.5), jnp.log(2.0)))
    col_scale = jnp.exp(jax.random.uniform(third, (1, 1, MODEL_WIDTH), jnp.float32, jnp.log(0.4), jnp.log(4.0)))
    base = jax.random.truncated_normal(first, -4.0, 4.0, (SEQS, SEQ_LEN, MODEL_WIDTH), jnp.float32)
    return (base * row_scale * col_scale).astype(jnp.bfloat16)


def draw_w_query(key, part):
    base_key = jax.random.fold_in(key, 23)
    first = jax.random.fold_in(base_key, 0)
    base = jax.random.truncated_normal(first, -4.0, 4.0, (MODEL_WIDTH, QUERY_HEADS * HEAD_SIZE), jnp.float32) / jnp.sqrt(MODEL_WIDTH * 1.0)
    return jnp.clip(base, -8.0, 8.0).astype(jnp.bfloat16)


def steps_of(own_key, dims, cuts, smallest, largest):
    level = 1.0
    for position, shards_of in cuts:
        draws = jax.random.uniform(jax.random.fold_in(jax.random.fold_in(own_key, 6), position), (shards_of,), jnp.float32, smallest / len(cuts), largest / len(cuts))
        level = level * jnp.repeat(jnp.exp(draws), dims[position] // shards_of).reshape((-1,) + (1,) * (len(dims) - 1 - position))
    return level


def gaussian(stream_key, shape, scale, reach, cuts=(), kind=jnp.bfloat16):
    factor_of = steps_of(stream_key, shape, cuts, -0.22, 0.18) if cuts else 1.0
    result = jax.random.normal(stream_key, shape, jnp.float32) * scale * factor_of
    return jnp.minimum(jnp.maximum(result, -reach), reach).astype(kind)


def setup_inputs(seed: int = 0) -> dict:
    seeds = jax.random.split(jax.random.key(seed), 11)
    block_input = draw_block_input(jax.random.fold_in(seeds[10], 71), 0)
    cotangent = gaussian(seeds[1], (SEQS, SEQ_LEN, MODEL_WIDTH), 1.0, 6.0, ((0, 8), (1, 4)))
    norm_gains = jnp.clip(1.0 + 0.18 * jax.random.normal(seeds[2], (2, MODEL_WIDTH), jnp.float32), 0.099609375, 1.8984375).astype(jnp.bfloat16)
    w_query = draw_w_query(jax.random.fold_in(seeds[10], 71), 0)
    key_weight = gaussian(seeds[4], (MODEL_WIDTH, KEY_VALUE_HEADS * HEAD_SIZE), MODEL_WIDTH ** -0.5, 0.1875, ((1, 4),))
    value_weight = gaussian(seeds[5], (MODEL_WIDTH, KEY_VALUE_HEADS * HEAD_SIZE), MODEL_WIDTH ** -0.5, 0.1875, ((1, 4),))
    w_out = gaussian(seeds[6], (QUERY_HEADS * HEAD_SIZE, MODEL_WIDTH), (QUERY_HEADS * HEAD_SIZE // 16) ** -0.5, 0.75, ((1, 4),))
    w_gate = gaussian(seeds[7], (MODEL_WIDTH, HIDDEN_UNITS), MODEL_WIDTH ** -0.5, 0.1875, ((1, 4),))
    w_up = gaussian(seeds[8], (MODEL_WIDTH, HIDDEN_UNITS), MODEL_WIDTH ** -0.5, 0.1875, ((1, 4),))
    w_down = gaussian(seeds[9], (HIDDEN_UNITS, MODEL_WIDTH), (HIDDEN_UNITS // 4) ** -0.5, 0.25, ((1, 4),))
    return {"block_input": block_input, "cotangent": cotangent, "norm_gains": norm_gains, "w_query": w_query, "key_weight": key_weight, "value_weight": value_weight, "w_out": w_out, "w_gate": w_gate, "w_up": w_up, "w_down": w_down}


EPS = 1e-05
THETA = 10000.0

def norm_scale(values):
    return lax.rsqrt(lax.optimization_barrier(jnp.mean(values * values, axis=-1, keepdims=True)) + EPS)

def rope_tables(block_start, token_rows):
    positions = (block_start + jnp.arange(token_rows, dtype=jnp.int32)).astype(jnp.float32)
    half = HEAD_SIZE // 2
    freq = jnp.exp(jnp.arange(half, dtype=jnp.int32).astype(jnp.float32) * (-2.0 * math.log(THETA) / HEAD_SIZE))
    angle = positions[:, None] * freq[None, :]
    return (jnp.cos(angle)[:, None, :], jnp.sin(angle)[:, None, :])

def apply_rotation(values, cosine_table, sine_table):
    half = values.shape[-1] // 2
    first = values[..., :half]
    second = values[..., half:]
    return jnp.concatenate([first * cosine_table - second * sine_table, second * cosine_table + first * sine_table], axis=-1)

def invert_rotation(values, cosine_table, sine_table):
    half = values.shape[-1] // 2
    first = values[..., :half]
    second = values[..., half:]
    return jnp.concatenate([first * cosine_table + second * sine_table, second * cosine_table - first * sine_table], axis=-1)

def plain_product(left, right):
    return jnp.dot(left, right, preferred_element_type=jnp.float32)

def dot_right(left, right):
    return jnp.dot(left, right.T, preferred_element_type=jnp.float32)

def dot_left(left, right):
    return jnp.dot(left.T, right, preferred_element_type=jnp.float32)

def attend_forward(queries, keys, values, allowed, scale):

    def one_head(items):
        qx, kx, vx = items
        scores = jnp.einsum('gcd,ld->gcl', qx.astype(jnp.float32), kx.astype(jnp.float32)) * scale
        scores = jnp.where(allowed[None], scores, -jnp.inf)
        peak = lax.optimization_barrier(jnp.max(scores, axis=-1, keepdims=True))
        total = lax.optimization_barrier(jnp.sum(jnp.exp(scores - peak), axis=-1, keepdims=True))
        logsum = peak + jnp.log(total)
        probs = jnp.exp(scores - logsum).astype(jnp.bfloat16)
        mixed = jnp.einsum('gcl,ld->gcd', probs.astype(jnp.float32), vx.astype(jnp.float32)).astype(jnp.bfloat16)
        return (mixed, logsum[..., 0])
    return lax.map(one_head, (queries, keys, values))

def attend_backward(queries, keys, values, grads, logsum, delta, allowed, scale):

    def one_head(items):
        qx, kx, vx, gx, lx, dx = items
        scores = jnp.einsum('gcd,ld->gcl', qx.astype(jnp.float32), kx.astype(jnp.float32)) * scale
        scores = jnp.where(allowed[None], scores, -jnp.inf)
        probs = jnp.exp(scores - lx[..., None])
        probs_low = probs.astype(jnp.bfloat16)
        dprobs = jnp.einsum('gcd,ld->gcl', gx.astype(jnp.float32), vx.astype(jnp.float32))
        dscores = (probs * (dprobs - dx[..., None]) * scale).astype(jnp.bfloat16)
        values_gradient = jnp.einsum('gcl,gcd->ld', probs_low.astype(jnp.float32), gx.astype(jnp.float32))
        dquery = jnp.einsum('gcl,ld->gcd', dscores.astype(jnp.float32), kx.astype(jnp.float32))
        keys_gradient = jnp.einsum('gcl,gcd->ld', dscores.astype(jnp.float32), qx.astype(jnp.float32))
        return (dquery, keys_gradient, values_gradient)
    return lax.map(one_head, (queries, keys, values, grads, logsum, delta))

def reference(block_input, cotangent, norm_gains, w_query, key_weight, value_weight, w_out, w_gate, w_up, w_down):
    block_length = SEQ_LEN
    query_groups = QUERY_HEADS // KEY_VALUE_HEADS
    scale = 1.0 / math.sqrt(HEAD_SIZE)
    gain_attn = norm_gains[0].astype(jnp.float32)
    gain_ffn = norm_gains[1].astype(jnp.float32)
    cosine_table, sine_table = rope_tables(0, block_length)
    places = jnp.arange(block_length, dtype=jnp.int32)
    allowed = places[None, :] <= places[:, None]

    def one_sequence(totals, item):
        x_seq, dy_seq = item
        xf = x_seq.astype(jnp.float32)
        r1 = norm_scale(xf)
        n1 = xf * r1
        first_activation = (n1 * gain_attn).astype(jnp.bfloat16)
        query_float = apply_rotation(plain_product(first_activation, w_query).reshape(block_length, QUERY_HEADS, HEAD_SIZE), cosine_table, sine_table).astype(jnp.bfloat16)
        key_float = apply_rotation(plain_product(first_activation, key_weight).reshape(block_length, KEY_VALUE_HEADS, HEAD_SIZE), cosine_table, sine_table).astype(jnp.bfloat16)
        value_float = plain_product(first_activation, value_weight).astype(jnp.bfloat16).reshape(block_length, KEY_VALUE_HEADS, HEAD_SIZE)
        query_heads = query_float.reshape(block_length, KEY_VALUE_HEADS, query_groups, HEAD_SIZE).transpose(1, 2, 0, 3)
        key_heads = key_float.transpose(1, 0, 2)
        value_heads = value_float.transpose(1, 0, 2)
        mixed, logsum = attend_forward(query_heads, key_heads, value_heads, allowed, scale)
        mixed_flat = mixed.transpose(2, 0, 1, 3).reshape(block_length, QUERY_HEADS * HEAD_SIZE)
        x2 = xf + plain_product(mixed_flat, w_out)
        r2 = norm_scale(x2)
        n2 = x2 * r2
        a2 = (n2 * gain_ffn).astype(jnp.bfloat16)
        gate = plain_product(a2, w_gate)
        up = plain_product(a2, w_up)
        sig = jax.nn.sigmoid(gate)
        act = gate * sig
        hidden = (act * up).astype(jnp.bfloat16)
        out = x2 + plain_product(hidden, w_down)
        dyf = dy_seq.astype(jnp.float32)
        d_hidden = dot_right(dy_seq, w_down)
        g_down = dot_left(hidden, dy_seq)
        d_gate = (d_hidden * up * sig * (1.0 + gate * (1.0 - sig))).astype(jnp.bfloat16)
        d_up = (d_hidden * act).astype(jnp.bfloat16)
        g_gate = dot_left(a2, d_gate)
        g_up = dot_left(a2, d_up)
        d_a2 = dot_right(d_gate, w_gate) + dot_right(d_up, w_up)
        g_ffn = lax.optimization_barrier(jnp.sum(d_a2 * n2, axis=0))
        d_n2 = d_a2 * gain_ffn
        d_x2 = dyf + r2 * (d_n2 - n2 * lax.optimization_barrier(jnp.mean(d_n2 * n2, axis=-1, keepdims=True)))
        d_x2_low = d_x2.astype(jnp.bfloat16)
        g_out = dot_left(mixed_flat, d_x2_low)
        mixed_gradient = dot_right(d_x2_low, w_out).astype(jnp.bfloat16)
        heads_gradient = mixed_gradient.reshape(block_length, KEY_VALUE_HEADS, query_groups, HEAD_SIZE).transpose(1, 2, 0, 3)
        delta = lax.optimization_barrier(jnp.sum(heads_gradient.astype(jnp.float32) * mixed.astype(jnp.float32), axis=-1))
        dquery, keys_gradient, values_gradient = attend_backward(query_heads, key_heads, value_heads, heads_gradient, logsum, delta, allowed, scale)
        dq = invert_rotation(dquery.transpose(2, 0, 1, 3).reshape(block_length, QUERY_HEADS, HEAD_SIZE), cosine_table, sine_table)
        dq = dq.reshape(block_length, QUERY_HEADS * HEAD_SIZE).astype(jnp.bfloat16)
        key_gradient = invert_rotation(keys_gradient.transpose(1, 0, 2), cosine_table, sine_table).reshape(block_length, KEY_VALUE_HEADS * HEAD_SIZE).astype(jnp.bfloat16)
        value_gradient = values_gradient.transpose(1, 0, 2).reshape(block_length, KEY_VALUE_HEADS * HEAD_SIZE).astype(jnp.bfloat16)
        g_query = dot_left(first_activation, dq)
        g_key = dot_left(first_activation, key_gradient)
        g_value = dot_left(first_activation, value_gradient)
        d_a1 = dot_right(dq, w_query) + dot_right(key_gradient, key_weight) + dot_right(value_gradient, value_weight)
        g_attn = lax.optimization_barrier(jnp.sum(d_a1 * n1, axis=0))
        d_n1 = d_a1 * gain_attn
        d_x = d_x2 + r1 * (d_n1 - n1 * lax.optimization_barrier(jnp.mean(d_n1 * n1, axis=-1, keepdims=True)))
        terms = (jnp.stack([g_attn, g_ffn]), g_query, g_key, g_value, g_out, g_gate, g_up, g_down)
        totals = tuple((old + new for old, new in zip(totals, terms)))
        return (totals, (out, d_x))
    block_start = (jnp.zeros((2, MODEL_WIDTH), jnp.float32), jnp.zeros((MODEL_WIDTH, QUERY_HEADS * HEAD_SIZE), jnp.float32), jnp.zeros((MODEL_WIDTH, KEY_VALUE_HEADS * HEAD_SIZE), jnp.float32), jnp.zeros((MODEL_WIDTH, KEY_VALUE_HEADS * HEAD_SIZE), jnp.float32), jnp.zeros((QUERY_HEADS * HEAD_SIZE, MODEL_WIDTH), jnp.float32), jnp.zeros((MODEL_WIDTH, HIDDEN_UNITS), jnp.float32), jnp.zeros((MODEL_WIDTH, HIDDEN_UNITS), jnp.float32), jnp.zeros((HIDDEN_UNITS, MODEL_WIDTH), jnp.float32))
    totals, outputs = lax.scan(one_sequence, block_start, (block_input, cotangent))
    block_output, input_grad = outputs
    return (block_output, input_grad, totals[0], totals[1], totals[2], totals[3], totals[4], totals[5], totals[6], totals[7])
```

```python
import math

import jax
import jax.numpy as jnp
import numpy as np
from jax import lax
from jax.sharding import PartitionSpec as P

HEAD_SIZE = 64
QUERY_HEADS = 15
KEY_VALUE_HEADS = 5
GROUP_QUERIES = QUERY_HEADS // KEY_VALUE_HEADS
EPS = 1e-05
THETA = 10000.0

BLOCK_ORDER = (0, 3, 1, 2)
PLACE_OF_BLOCK = (0, 2, 3, 1)

CORE_SWAP = [(0, 1), (1, 0), (2, 3), (3, 2)]
CHIP_SWAP = [(0, 2), (2, 0), (1, 3), (3, 1)]
CROSS_SWAP = [(0, 3), (3, 0), (1, 2), (2, 1)]


def norm_scale(values):
    return lax.rsqrt(jnp.mean(values * values, axis=-1, keepdims=True) + EPS)


def rope_tables(positions):
    half = HEAD_SIZE // 2
    freq = jnp.exp(
        jnp.arange(half, dtype=jnp.int32).astype(jnp.float32) * (-2.0 * math.log(THETA) / HEAD_SIZE)
    )
    angle = positions.astype(jnp.float32)[:, None] * freq[None, :]
    return (jnp.cos(angle)[:, None, :], jnp.sin(angle)[:, None, :])


def rotate(values, cosine, sine):
    half = values.shape[-1] // 2
    first = values[..., :half]
    second = values[..., half:]
    return jnp.concatenate([first * cosine - second * sine, second * cosine + first * sine], axis=-1)


def dot_nn(left, right):
    return jnp.dot(left, right, preferred_element_type=jnp.float32)


def dot_nt(left, right):
    return lax.dot_general(
        left, right, (((1,), (1,)), ((), ())), preferred_element_type=jnp.float32
    )


def dot_tn(left, right):
    return lax.dot_general(
        left, right, (((0,), (0,)), ((), ())), preferred_element_type=jnp.float32
    )


def gather_parts(part):
    across = lax.ppermute(part, "grp", CHIP_SWAP)
    beside = lax.ppermute(part, "grp", CORE_SWAP)
    corner = lax.ppermute(across, "grp", CORE_SWAP)
    return (part, beside, across, corner)


def exchange_parts(pieces, me):
    take = lambda k: lax.dynamic_index_in_dim(pieces, me ^ k, 0, keepdims=False)
    return (
        take(0),
        lax.ppermute(take(1), "grp", CORE_SWAP),
        lax.ppermute(take(2), "grp", CHIP_SWAP),
        lax.ppermute(take(3), "grp", CROSS_SWAP),
    )


def in_order(parts, me, order, axis):
    out = []
    for device in order:
        choice = parts[3]
        for k in (2, 1, 0):
            choice = jnp.where((me ^ k) == device, parts[k], choice)
        out.append(choice)
    return jnp.concatenate(out, axis=axis)


def sum_over_rep(partial):
    count = lax.axis_size("rep")
    bits = count.bit_length() - 1
    assert 1 << bits == count
    rows, columns = partial.shape
    me = lax.axis_index("rep")
    held = partial.reshape((2,) * bits + (rows // count, columns))
    for bit in range(bits):
        axis = bits - 1 - bit
        mine = (me >> bit) & 1
        away = lax.dynamic_index_in_dim(held, 1 - mine, axis, keepdims=False).astype(jnp.bfloat16)
        came = lax.ppermute(away, "rep", [(i, i ^ (1 << bit)) for i in range(count)])
        held = lax.dynamic_index_in_dim(held, mine, axis, keepdims=False) + came.astype(jnp.float32)
    return held


def per_device(
    block_input,
    cotangent,
    norm_gains,
    w_query,
    key_weight,
    value_weight,
    w_out,
    w_gate,
    w_up,
    w_down,
):
    bf16 = jnp.bfloat16
    me = lax.axis_index("grp")
    rows = block_input.shape[1]
    width = block_input.shape[2]
    half_rows = 2 * rows
    kv_width = KEY_VALUE_HEADS * HEAD_SIZE
    slice_width = w_query.shape[1]
    hidden_slice = w_gate.shape[1]
    scale = 1.0 / math.sqrt(HEAD_SIZE)
    second_set = ((me == 1) | (me == 2)).astype(jnp.int32)
    own_start = second_set * half_rows
    beside_start = half_rows - own_start

    places = np.concatenate([np.arange(b * rows, (b + 1) * rows, dtype=np.int32) for b in BLOCK_ORDER])
    all_positions = jnp.asarray(places)
    own_positions = lax.dynamic_slice_in_dim(all_positions, own_start, half_rows)

    def own_half(values):
        return lax.dynamic_slice_in_dim(values, own_start, half_rows, 0)

    def two_halves(own):
        beside = lax.ppermute(own, "grp", CORE_SWAP)
        first = jnp.where(second_set == 1, beside, own)
        second = jnp.where(second_set == 1, own, beside)
        return jnp.concatenate([first, second], axis=0)

    x_parts = gather_parts(block_input[0])
    gain_parts = gather_parts(norm_gains.T)
    qkv_t = jnp.concatenate([w_query.T, key_weight.T, value_weight.T], axis=0)
    qkv_parts = gather_parts(qkv_t)
    wo_parts = gather_parts(w_out.T)
    dy_parts = gather_parts(cotangent[0])
    down_t = w_down.T.reshape(slice_width, 4, hidden_slice).transpose(1, 0, 2)
    down_parts = exchange_parts(down_t, me)

    x_all = in_order(x_parts, me, BLOCK_ORDER, 0)
    dy_all = in_order(dy_parts, me, BLOCK_ORDER, 0)
    gains = in_order(gain_parts, me, range(4), 0).astype(jnp.float32)
    gain_attn = gains[:, 0]
    gain_ffn = gains[:, 1]
    kv_slice = key_weight.shape[1]
    wq_t = in_order([p[:slice_width] for p in qkv_parts], me, range(4), 0)
    wk_t = in_order([p[slice_width : slice_width + kv_slice] for p in qkv_parts], me, range(4), 0)
    wv_t = in_order([p[slice_width + kv_slice :] for p in qkv_parts], me, range(4), 0)
    wo_t = in_order(wo_parts, me, range(4), 0)
    down_rows_t = in_order(down_parts, me, range(4), 0)

    xf = x_all.astype(jnp.float32)
    r1 = norm_scale(xf)
    a1 = (xf * r1 * gain_attn).astype(bf16)
    a1_own = own_half(a1)
    cos_all, sin_all = rope_tables(all_positions)
    cos_own, sin_own = rope_tables(own_positions)
    q = rotate(dot_nt(a1_own, wq_t).reshape(half_rows, QUERY_HEADS, HEAD_SIZE), cos_own, sin_own).astype(bf16)
    k = rotate(dot_nt(a1, wk_t).reshape(4 * rows, KEY_VALUE_HEADS, HEAD_SIZE), cos_all, sin_all).astype(bf16)
    v = dot_nt(a1, wv_t).astype(bf16).reshape(4 * rows, KEY_VALUE_HEADS, HEAD_SIZE)
    q = q.reshape(half_rows, KEY_VALUE_HEADS, GROUP_QUERIES, HEAD_SIZE).transpose(1, 2, 0, 3)
    k = k.transpose(1, 0, 2)
    v = v.transpose(1, 0, 2)
    allowed = all_positions[None, :] <= own_positions[:, None]
    scores = jnp.einsum("hgcd,hld->hgcl", q, k, preferred_element_type=jnp.float32) * scale
    scores = jnp.where(allowed, scores, -jnp.inf)
    peak = jnp.max(scores, axis=-1, keepdims=True)
    logsum = peak + jnp.log(jnp.sum(jnp.exp(scores - peak), axis=-1, keepdims=True))
    probs = jnp.exp(scores - logsum)
    probs_low = probs.astype(bf16)
    mixed = jnp.einsum("hgcl,hld->hgcd", probs_low, v, preferred_element_type=jnp.float32).astype(bf16)
    o_own = mixed.transpose(2, 0, 1, 3).reshape(half_rows, width)

    x2 = own_half(xf) + dot_nt(o_own, wo_t)
    r2 = norm_scale(x2)
    n2 = x2 * r2
    a2 = two_halves((n2 * gain_ffn).astype(bf16))

    gate = dot_nn(a2, w_gate)
    up = dot_nn(a2, w_up)
    sig = jax.nn.sigmoid(gate)
    act = gate * sig
    hidden = (act * up).astype(bf16)
    d_hidden = dot_nn(dy_all, down_rows_t)
    d_gate = (d_hidden * up * sig * (1.0 + gate * (1.0 - sig))).astype(bf16)
    d_up = (d_hidden * act).astype(bf16)
    d_a2_part = (dot_nt(d_gate, w_gate) + dot_nt(d_up, w_up)).astype(bf16)
    g_gate = sum_over_rep(dot_tn(a2, d_gate))
    g_up = sum_over_rep(dot_tn(a2, d_up))

    beside_part = lax.ppermute(
        lax.dynamic_slice_in_dim(d_a2_part, beside_start, half_rows, 0), "grp", CORE_SWAP
    )
    chip_sum = own_half(d_a2_part).astype(jnp.float32) + beside_part.astype(jnp.float32)
    d_a2 = chip_sum + lax.ppermute(chip_sum.astype(bf16), "grp", CROSS_SWAP).astype(jnp.float32)

    hidden_all = in_order(gather_parts(hidden), me, range(4), 1)
    own_columns = lax.dynamic_slice_in_dim(dy_all, 0, 4 * rows, 0)
    dy_columns = jnp.concatenate(
        [lax.dynamic_slice_in_dim(own_columns, me * slice_width, slice_width, 1)], axis=1
    )
    g_down = sum_over_rep(dot_tn(hidden_all, dy_columns))
    out_columns = dot_nn(hidden_all, w_down).astype(bf16).reshape(4, rows, slice_width)
    out_columns = jnp.stack([out_columns[PLACE_OF_BLOCK[b]] for b in range(4)])
    out_rows = in_order(exchange_parts(out_columns, me), me, range(4), 1)
    first_block = (me < 2).astype(jnp.int32) * 0
    own_block_start = jnp.where((me == 0) | (me == 1), 0, rows)

    def own_block(values):
        return lax.dynamic_slice_in_dim(values, own_block_start, rows, 0)

    block_output = own_block(x2) + out_rows.astype(jnp.float32)

    dyf = own_half(dy_all).astype(jnp.float32)
    d_n2 = d_a2 * gain_ffn
    d_x2 = dyf + r2 * (d_n2 - n2 * jnp.mean(d_n2 * n2, axis=-1, keepdims=True))
    d_x2_low = d_x2.astype(bf16)
    g_ffn = jnp.sum(own_block(d_a2 * n2), axis=0)
    o_all = two_halves(o_own)

    def column_halves(own):
        away = lax.dynamic_slice_in_dim(own, (me ^ 1) * (own.shape[1] // 4), own.shape[1] // 4, 1)
        kept = lax.dynamic_slice_in_dim(own, me * (own.shape[1] // 4), own.shape[1] // 4, 1)
        came = lax.ppermute(away, "grp", CORE_SWAP)
        first = jnp.where(second_set == 1, came, kept)
        second = jnp.where(second_set == 1, kept, came)
        return jnp.concatenate([first, second], axis=0)

    g_out = sum_over_rep(dot_tn(o_all, column_halves(d_x2_low)))

    d_o = dot_nn(d_x2_low, wo_t).astype(bf16)
    d_o = d_o.reshape(half_rows, KEY_VALUE_HEADS, GROUP_QUERIES, HEAD_SIZE).transpose(1, 2, 0, 3)
    delta = jnp.sum(d_o.astype(jnp.float32) * mixed.astype(jnp.float32), axis=-1, keepdims=True)
    d_probs = jnp.einsum("hgcd,hld->hgcl", d_o, v, preferred_element_type=jnp.float32)
    d_scores = (probs * (d_probs - delta) * scale).astype(bf16)
    d_v = jnp.einsum("hgcl,hgcd->hld", probs_low, d_o, preferred_element_type=jnp.float32)
    d_q = jnp.einsum("hgcl,hld->hgcd", d_scores, k, preferred_element_type=jnp.float32)
    d_k = jnp.einsum("hgcl,hgcd->hld", d_scores, q, preferred_element_type=jnp.float32)
    d_kv = jnp.stack([d_k, d_v])
    d_kv = d_kv + lax.ppermute(d_kv, "grp", CORE_SWAP)
    d_q = rotate(d_q.transpose(2, 0, 1, 3).reshape(half_rows, QUERY_HEADS, HEAD_SIZE), cos_own, -sin_own)
    d_q = d_q.reshape(half_rows, width).astype(bf16)
    d_k = rotate(d_kv[0].transpose(1, 0, 2), cos_all, -sin_all).reshape(4 * rows, kv_width).astype(bf16)
    d_v = d_kv[1].transpose(1, 0, 2).reshape(4 * rows, kv_width).astype(bf16)

    def own_cols(values):
        return lax.dynamic_slice_in_dim(values, me * (values.shape[1] // 4), values.shape[1] // 4, 1)

    d_mine = jnp.concatenate([column_halves(d_q), own_cols(d_k), own_cols(d_v)], axis=1)
    g_qkv = sum_over_rep(dot_tn(a1, d_mine))
    d_q_block, d_k_block, d_v_block = own_block(d_q), own_block(own_half(d_k)), own_block(own_half(d_v))
    d_a1 = dot_nn(d_q_block, wq_t) + dot_nn(d_k_block, wk_t) + dot_nn(d_v_block, wv_t)
    x_block = block_input[0].astype(jnp.float32)
    r1_block = norm_scale(x_block)
    n1_block = x_block * r1_block
    g_attn = jnp.sum(d_a1 * n1_block, axis=0)
    d_n1 = d_a1 * gain_attn
    input_grad = own_block(d_x2) + r1_block * (
        d_n1 - n1_block * jnp.mean(d_n1 * n1_block, axis=-1, keepdims=True)
    )
    g_gains = lax.psum(jnp.stack([g_attn, g_ffn]), ("rep", "grp"))
    g_gains = lax.dynamic_slice_in_dim(g_gains, me * slice_width, slice_width, 1)
    return (
        block_output[None],
        input_grad[None],
        g_gains,
        g_qkv[:, :slice_width],
        g_qkv[:, slice_width : slice_width + kv_slice],
        g_qkv[:, slice_width + kv_slice :],
        g_out,
        g_gate,
        g_up,
        g_down,
    )


def solution(mesh):
    rows = P("rep", "grp", None)
    weight = P(None, "grp")
    grad = P("rep", "grp")
    return jax.shard_map(
        per_device,
        mesh=mesh,
        in_specs=(rows, rows) + (weight,) * 8,
        out_specs=(rows, rows, weight) + (grad,) * 7,
        check_vma=False,
    )
```

```python
import math

import jax
import jax.numpy as jnp
import numpy as np
from jax import lax
from jax.experimental.layout import Layout, with_layout_constraint
from jax.sharding import PartitionSpec as P

HEAD_SIZE = 64
QUERY_HEADS = 15
KEY_VALUE_HEADS = 5
GROUP_QUERIES = QUERY_HEADS // KEY_VALUE_HEADS
EPS = 1e-05
THETA = 10000.0

BLOCK_ORDER = (0, 3, 1, 2)

CORE_SWAP = [(0, 1), (1, 0), (2, 3), (3, 2)]
CHIP_SWAP = [(0, 2), (2, 0), (1, 3), (3, 1)]
CROSS_SWAP = [(0, 3), (3, 0), (1, 2), (2, 1)]


def norm_scale(values):
    return lax.rsqrt(jnp.mean(values * values, axis=-1, keepdims=True) + EPS)


def rope_tables(positions):
    half = HEAD_SIZE // 2
    freq = jnp.exp(
        jnp.arange(half, dtype=jnp.int32).astype(jnp.float32) * (-2.0 * math.log(THETA) / HEAD_SIZE)
    )
    angle = positions.astype(jnp.float32)[:, None] * freq[None, :]
    return (jnp.cos(angle)[:, None, :], jnp.sin(angle)[:, None, :])


def rotate(values, cosine, sine):
    half = values.shape[-1] // 2
    first = values[..., :half]
    second = values[..., half:]
    return jnp.concatenate([first * cosine - second * sine, second * cosine + first * sine], axis=-1)


def dot_nn(left, right):
    return jnp.dot(left, right, preferred_element_type=jnp.float32)


def dot_nt(left, right):
    return lax.dot_general(
        left, right, (((1,), (1,)), ((), ())), preferred_element_type=jnp.float32
    )


def dot_tn(left, right):
    return lax.dot_general(
        left, right, (((0,), (0,)), ((), ())), preferred_element_type=jnp.float32
    )


def after(value, *tokens):
    return lax.optimization_barrier((value,) + tokens)[0]


class Order:
    def __init__(self):
        self.token = None

    def mark(self, value):
        self.token = value

    def hold(self, *values):
        if self.token is None:
            return values if len(values) > 1 else values[0]
        held = lax.optimization_barrier(values + (self.token,))[:-1]
        return held if len(held) > 1 else held[0]


def rep_bits():
    count = lax.axis_size("rep")
    bits = count.bit_length() - 1
    assert 1 << bits == count and bits >= 3
    return bits


def swap_over_rep(held, bit, axis):
    count = lax.axis_size("rep")
    mine = (lax.axis_index("rep") >> bit) & 1
    away = lax.dynamic_index_in_dim(held, 1 - mine, axis, keepdims=False).astype(jnp.bfloat16)
    came = lax.ppermute(away, "rep", [(i, i ^ (1 << bit)) for i in range(count)])
    return lax.dynamic_index_in_dim(held, mine, axis, keepdims=False), came, away


def joined(pair):
    return pair[0] + pair[1].astype(jnp.float32)


class RepSum:
    def __init__(self, partial, order):
        bits = rep_bits()
        self.bits_to_go = list(order) + list(range(len(order), bits))
        self.left = list(range(bits))
        self.held = partial.reshape((2,) * bits + partial.shape[1:])
        self.step()

    def step(self):
        bit = self.bits_to_go.pop(0)
        axis = len(self.left) - 1 - self.left.index(bit)
        self.left.remove(bit)
        self.kept, self.came, self.sent = swap_over_rep(self.held, bit, axis)

    def next(self, order):
        self.held = joined((self.kept, order.hold(self.came)))
        self.step()
        order.mark(self.sent)

    def end(self, order):
        while self.bits_to_go:
            self.next(order)
        return joined((self.kept, order.hold(self.came)))


def by_rep(partial):
    count = lax.axis_size("rep")
    return partial.reshape((count, partial.shape[0] // count) + partial.shape[1:])


def per_device(
    block_input,
    cotangent,
    norm_gains,
    w_query,
    key_weight,
    value_weight,
    w_out,
    w_gate,
    w_up,
    w_down,
):
    bf16 = jnp.bfloat16
    me = lax.axis_index("grp")
    rows = block_input.shape[1]
    width = block_input.shape[2]
    half_rows = 2 * rows
    kv_width = KEY_VALUE_HEADS * HEAD_SIZE
    slice_width = w_query.shape[1]
    kv_slice = key_weight.shape[1]
    hidden_slice = w_gate.shape[1]
    scale = 1.0 / math.sqrt(HEAD_SIZE)
    second_set = (me == 1) | (me == 2)
    own_start = second_set.astype(jnp.int32) * half_rows
    beside_start = half_rows - own_start
    own_block_start = jnp.where(me < 2, 0, rows)

    def own_half(values):
        return lax.dynamic_slice_in_dim(values, own_start, half_rows, 0)

    def own_block(values):
        return lax.dynamic_slice_in_dim(values, own_block_start, rows, 0)

    def own_cols(values):
        return lax.dynamic_slice_in_dim(values, me * (values.shape[1] // 4), values.shape[1] // 4, 1)

    def in_pair(own, cross):
        return jnp.concatenate([jnp.where(me < 2, own, cross), jnp.where(me < 2, cross, own)], axis=0)

    def sets(own, beside):
        return jnp.where(second_set, beside, own), jnp.where(second_set, own, beside)

    def core_swap(values):
        return lax.ppermute(values, "grp", CORE_SWAP)

    def chip_cross(values):
        return lax.ppermute(values, "grp", CROSS_SWAP)

    def two_halves(own, beside):
        return jnp.concatenate(sets(own, beside), axis=0)

    def in_order(own, beside, cross, corner, order=(0, 1, 2, 3)):
        out = []
        for device in order:
            out.append(
                jnp.where(
                    me == device,
                    own,
                    jnp.where(me == device ^ 1, beside, jnp.where(me == device ^ 3, cross, corner)),
                )
            )
        return jnp.concatenate(out, axis=0)

    turn = Order()

    x_cross = chip_cross(block_input[0])
    qkv_sent = jnp.concatenate(
        [
            w_query.T,
            key_weight.T,
            value_weight.T,
            jnp.pad(norm_gains, ((0, 6), (0, width - slice_width))),
        ],
        axis=0,
    )
    qkv_cross = chip_cross(qkv_sent)
    turn.mark(qkv_sent)
    qkv_beside = core_swap(turn.hold(qkv_sent))
    places = np.concatenate([np.arange(b * rows, (b + 1) * rows, dtype=np.int32) for b in BLOCK_ORDER])
    all_positions = turn.hold(jnp.asarray(places))
    own_positions = own_half(all_positions)
    cos_all, sin_all = rope_tables(all_positions)
    cos_own, sin_own = rope_tables(own_positions)
    allowed = all_positions[None, :] <= own_positions[:, None]
    wo_sent = turn.hold(w_out).T
    dy_here, down_t = turn.hold(cotangent, w_down)
    dy_here = dy_here[0]
    down_t = down_t.T
    wo_beside = core_swap(wo_sent)
    dy_beside = core_swap(dy_here)

    def down_piece(k):
        return lax.dynamic_slice_in_dim(down_t, (me ^ k) * hidden_slice, hidden_slice, 1)

    down_pieces = [down_piece(k) for k in range(4)]
    down_beside = core_swap(down_pieces[1])
    cos_all, sin_all, cos_own, sin_own, allowed, wo_sent, down_0, down_2, down_3 = lax.optimization_barrier(
        (cos_all, sin_all, cos_own, sin_own, allowed, wo_sent, down_pieces[0], down_pieces[2], down_pieces[3])
    )
    turn.mark(down_3)

    xf = in_pair(block_input[0], turn.hold(x_cross)).astype(jnp.float32)
    r1 = norm_scale(xf)
    n1 = xf * r1
    turn.mark(r1)
    qkv_cross = turn.hold(qkv_cross)
    qkv_corner = core_swap(qkv_cross)
    turn.mark(qkv_cross)
    wo_cross = chip_cross(turn.hold(wo_sent))
    dy_cross = chip_cross(turn.hold(dy_here))
    down_across = lax.ppermute(turn.hold(down_2), "grp", CHIP_SWAP)
    down_cross = chip_cross(turn.hold(down_3))
    qkv_all = (qkv_sent, qkv_beside, qkv_cross, qkv_corner)

    def rows_of_all(start, size):
        return in_order(*(part[start : start + size] for part in qkv_all))

    gain_row = slice_width + 2 * kv_slice
    gains = rows_of_all(gain_row, 8).reshape(4, 8, width)[:, :2, :slice_width]
    gains = gains.transpose(1, 0, 2).reshape(2, width).astype(jnp.float32)
    gain_attn = gains[0]
    gain_ffn = gains[1]
    a1_own = (n1 * gain_attn).astype(bf16)
    a1 = two_halves(a1_own, core_swap(a1_own))
    wq_t = rows_of_all(0, slice_width)
    wk_t = rows_of_all(slice_width, kv_slice)
    wv_t = rows_of_all(slice_width + kv_slice, kv_slice)

    k = rotate(dot_nt(a1, wk_t).reshape(4 * rows, KEY_VALUE_HEADS, HEAD_SIZE), cos_all, sin_all).astype(bf16)
    v = dot_nt(a1, wv_t).astype(bf16).reshape(4 * rows, KEY_VALUE_HEADS, HEAD_SIZE)
    k = k.transpose(1, 0, 2)
    v = v.transpose(1, 0, 2)
    q = rotate(dot_nt(a1_own, wq_t).reshape(half_rows, QUERY_HEADS, HEAD_SIZE), cos_own, sin_own).astype(bf16)
    q = q.reshape(half_rows, KEY_VALUE_HEADS, GROUP_QUERIES, HEAD_SIZE).transpose(1, 2, 0, 3)
    scores = jnp.einsum("hgcd,hld->hgcl", q, k, preferred_element_type=jnp.float32) * scale
    scores = jnp.where(allowed, scores, -jnp.inf)
    peak = jnp.max(scores, axis=-1, keepdims=True)
    logsum = peak + jnp.log(jnp.sum(jnp.exp(scores - peak), axis=-1, keepdims=True))
    probs = jnp.exp(scores - logsum)
    probs_low = probs.astype(bf16)
    mixed = jnp.einsum("hgcl,hld->hgcd", probs_low, v, preferred_element_type=jnp.float32).astype(bf16)
    o_own = mixed.transpose(2, 0, 1, 3).reshape(half_rows, width)
    turn.mark(o_own)

    wo_cross, dy_cross = turn.hold(wo_cross, dy_cross)
    wo_t = in_order(wo_sent, wo_beside, wo_cross, core_swap(wo_cross))
    x2 = xf + dot_nt(o_own, wo_t)
    r2 = norm_scale(x2)
    n2 = x2 * r2
    a2_own = (n2 * gain_ffn).astype(bf16)
    a2_beside = core_swap(a2_own)
    turn.mark(a2_own)
    down_across = turn.hold(down_across)
    dy_all = in_order(dy_here, dy_beside, dy_cross, core_swap(dy_cross), BLOCK_ORDER)
    a2 = two_halves(a2_own, a2_beside)

    gate = dot_nn(a2, w_gate)
    up = dot_nn(a2, w_up)
    gate, up, dy_all, down_across = lax.optimization_barrier((gate, up, dy_all, down_across))
    turn.mark(up)
    o_beside = core_swap(turn.hold(o_own))
    sig = jax.nn.sigmoid(gate)
    act = gate * sig
    hidden = (act * up).astype(bf16)
    down_cross = turn.hold(down_cross)
    down_rows_t = in_order(down_0, down_beside, down_cross, down_across)
    d_hidden = dot_nn(dy_all, down_rows_t)
    d_gate = (d_hidden * up * sig * (1.0 + gate * (1.0 - sig))).astype(bf16)
    d_up = (d_hidden * act).astype(bf16)
    d_a2_part = (dot_nt(d_gate, w_gate) + dot_nt(d_up, w_up)).astype(bf16)

    beside_part = core_swap(lax.dynamic_slice_in_dim(d_a2_part, beside_start, half_rows, 0))
    chip_sum = own_half(d_a2_part).astype(jnp.float32) + beside_part.astype(jnp.float32)
    chip_sent = chip_sum.astype(bf16)
    other_chip = chip_cross(chip_sent)
    turn.mark(chip_sent)
    a2_late, d_gate, d_up, hidden = turn.hold(a2, d_gate, d_up, hidden)
    gate_sum = RepSum(by_rep(dot_tn(a2_late, d_gate)), (0, 1))
    turn.mark(gate_sum.sent)
    up_sum = RepSum(by_rep(dot_tn(turn.hold(a2_late), d_up)), (1, 0))
    turn.mark(up_sum.sent)
    g_down = dot_tn(turn.hold(dy_all), hidden).reshape(2, 2, slice_width, hidden_slice)
    down_pair = swap_over_rep(g_down, 0, 1)
    turn.mark(down_pair[2])

    out_part = dot_nt(turn.hold(hidden), down_rows_t).astype(bf16)
    out_beside = core_swap(lax.dynamic_slice_in_dim(out_part, beside_start, half_rows, 0))
    out_chip = own_half(out_part).astype(jnp.float32) + out_beside.astype(jnp.float32)
    out_away = lax.dynamic_slice_in_dim(out_chip, rows - own_block_start, rows, 0).astype(bf16)
    turn.mark(out_away)

    other_chip = turn.hold(other_chip)
    d_a2 = chip_sum + other_chip.astype(jnp.float32)
    dyf = own_half(dy_all).astype(jnp.float32)
    d_n2 = d_a2 * gain_ffn
    d_x2 = dyf + r2 * (d_n2 - n2 * jnp.mean(d_n2 * n2, axis=-1, keepdims=True))
    d_x2_low = d_x2.astype(bf16)

    def column_parts(own):
        away = lax.dynamic_slice_in_dim(own, (me ^ 1) * slice_width, slice_width, 1)
        return own_cols(own), core_swap(away)

    d_o = dot_nn(d_x2_low, wo_t).astype(bf16)
    turn.mark(d_o)
    out_cross = chip_cross(turn.hold(out_away))
    up_sum.next(turn)
    d_o = turn.hold(d_o)
    d_o = d_o.reshape(half_rows, KEY_VALUE_HEADS, GROUP_QUERIES, HEAD_SIZE).transpose(1, 2, 0, 3)
    delta = jnp.sum(d_o.astype(jnp.float32) * mixed.astype(jnp.float32), axis=-1, keepdims=True)
    d_probs = jnp.einsum("hgcd,hld->hgcl", d_o, v, preferred_element_type=jnp.float32)
    d_scores = (probs * (d_probs - delta) * scale).astype(bf16)
    d_v = jnp.einsum("hgcl,hgcd->hld", probs_low, d_o, preferred_element_type=jnp.float32)
    d_k = jnp.einsum("hgcl,hgcd->hld", d_scores, q, preferred_element_type=jnp.float32)
    d_kv = jnp.concatenate([d_k, d_v], axis=0).transpose(1, 0, 2).reshape(4 * rows, 2 * kv_width)
    d_kv_sent = d_kv.astype(bf16)
    d_kv_beside = core_swap(d_kv_sent)
    turn.mark(d_kv_sent)
    d_scores = turn.hold(d_scores)
    d_q = jnp.einsum("hgcl,hld->hgcd", d_scores, k, preferred_element_type=jnp.float32)
    d_q = rotate(d_q.transpose(2, 0, 1, 3).reshape(half_rows, QUERY_HEADS, HEAD_SIZE), cos_own, -sin_own)
    d_q = d_q.reshape(half_rows, width).astype(bf16)
    d_q_columns = column_parts(d_q)
    turn.mark(d_q)
    gate_sum.next(turn)
    down_held = joined((down_pair[0], turn.hold(down_pair[1])))
    down_pair = swap_over_rep(down_held, 1, 0)
    turn.mark(down_pair[2])

    d_kv, d_kv_beside = turn.hold(d_kv, d_kv_beside)
    d_kv = d_kv + d_kv_beside.astype(jnp.float32)
    d_k = rotate(
        d_kv[:, :kv_width].reshape(4 * rows, KEY_VALUE_HEADS, HEAD_SIZE), cos_all, -sin_all
    ).reshape(4 * rows, kv_width).astype(bf16)
    d_v = d_kv[:, kv_width:].astype(bf16)
    d_a1 = (
        dot_nn(own_block(d_q), wq_t)
        + dot_nn(own_block(own_half(d_k)), wk_t)
        + dot_nn(own_block(own_half(d_v)), wv_t)
    )
    n1_block = own_block(n1)
    g_attn = jnp.sum(d_a1 * n1_block, axis=0)
    g_ffn = jnp.sum(own_block(d_a2 * n2), axis=0)
    g_gains = jnp.stack([g_attn, g_ffn]).reshape(2, 4, slice_width).transpose(1, 0, 2)

    def gain_piece(k):
        return lax.dynamic_index_in_dim(g_gains, me ^ k, 0, keepdims=False)

    gains_came = (
        core_swap(gain_piece(1)),
        lax.ppermute(gain_piece(2), "grp", CHIP_SWAP),
        chip_cross(gain_piece(3)),
    )
    turn.mark(g_gains)

    g_kv = by_rep(dot_tn(turn.hold(a1), jnp.concatenate([own_cols(d_k), own_cols(d_v)], axis=1)))
    g_q = by_rep(dot_tn(turn.hold(a1), two_halves(*d_q_columns)))
    g_out = by_rep(dot_tn(turn.hold(two_halves(o_own, o_beside)), two_halves(*column_parts(d_x2_low))))
    turn.mark(g_out)
    gains_came = turn.hold(*gains_came)
    g_gains = gain_piece(0) + gains_came[0] + gains_came[1] + gains_came[2]
    count = g_q.shape[0]
    share = g_q.shape[1]
    riders = jnp.broadcast_to(jnp.pad(g_gains, ((0, 6), (0, 0))), (count, 8, slice_width))
    g_kv = jnp.pad(g_kv, ((0, 0), (0, 0), (0, slice_width - 2 * kv_slice)))
    bundle = jnp.concatenate([g_q, g_out, g_kv, riders], axis=1)
    bundle = with_layout_constraint(bundle, Layout(major_to_minor=(0, 1, 2)))
    attn_sum = RepSum(bundle, (0, 1))
    turn.mark(attn_sum.sent)

    up_sum.next(turn)
    gate_sum.next(turn)
    down_held = joined((down_pair[0], turn.hold(down_pair[1])))
    parts = count // 4
    down_held = down_held.reshape(slice_width, parts, hidden_slice // parts).transpose(1, 0, 2)
    down_held = down_held.reshape((2,) * (parts.bit_length() - 1) + (slice_width, hidden_slice // parts))
    down_pair = swap_over_rep(down_held, rep_bits() - 1, 0)
    turn.mark(down_pair[2])

    attn_sum.next(turn)
    d_a1_late, d_x2_late = turn.hold(d_a1, d_x2)
    d_n1 = d_a1_late * gain_attn
    input_grad = own_block(d_x2_late) + own_block(r1) * (
        d_n1 - n1_block * jnp.mean(d_n1 * n1_block, axis=-1, keepdims=True)
    )
    block_output = own_block(x2) + own_block(out_chip) + turn.hold(out_cross).astype(jnp.float32)
    input_grad, block_output = lax.optimization_barrier((input_grad, block_output))
    turn.mark(block_output)

    down_held = joined((down_pair[0], turn.hold(down_pair[1])))
    for bit in reversed(range(2, rep_bits() - 1)):
        down_held = joined(swap_over_rep(down_held, bit, 0))
    homes = [
        (j * count + r, (r & 3) * count + j * parts + (r >> 2)) for r in range(count) for j in range(4)
    ]
    down_sent = down_held.astype(bf16)
    g_down = lax.ppermute(down_sent, ("grp", "rep"), homes)
    turn.mark(down_sent)
    attn_sum.next(turn)
    g_gate = gate_sum.end(turn)
    g_up = up_sum.end(turn)
    g_down = turn.hold(g_down).astype(jnp.float32).T
    g_gate, g_up, g_down = lax.optimization_barrier((g_gate, g_up, g_down))
    turn.mark(g_down)
    g_attn_w = attn_sum.end(turn)
    g_kv = g_attn_w[2 * share : 3 * share]
    return (
        block_output[None],
        input_grad[None],
        g_attn_w[3 * share : 3 * share + 2],
        g_attn_w[:share],
        g_kv[:, :kv_slice],
        g_kv[:, kv_slice : 2 * kv_slice],
        g_attn_w[share : 2 * share],
        g_gate,
        g_up,
        g_down,
    )


def solution(mesh):
    rows = P("rep", "grp", None)
    weight = P(None, "grp")
    grad = P("rep", "grp")
    return jax.shard_map(
        per_device,
        mesh=mesh,
        in_specs=(rows, rows) + (weight,) * 8,
        out_specs=(rows, rows, weight) + (grad,) * 7,
        check_vma=False,
    )
```

```python
import math

import jax
import jax.numpy as jnp
import numpy as np
from jax import lax
from jax.experimental.layout import Layout, with_layout_constraint
from jax.experimental import pallas as pl
from jax.experimental.pallas import tpu as pltpu
from jax.sharding import PartitionSpec as P

HEAD_SIZE = 64
QUERY_HEADS = 15
KEY_VALUE_HEADS = 5
GROUP_QUERIES = QUERY_HEADS // KEY_VALUE_HEADS
EPS = 1e-05
THETA = 10000.0

BLOCK_ORDER = (0, 3, 1, 2)

CORE_SWAP = [(0, 1), (1, 0), (2, 3), (3, 2)]
CHIP_SWAP = [(0, 2), (2, 0), (1, 3), (3, 1)]
CROSS_SWAP = [(0, 3), (3, 0), (1, 2), (2, 1)]


def norm_scale(values):
    return lax.rsqrt(jnp.mean(values * values, axis=-1, keepdims=True) + EPS)


def rope_tables(positions):
    half = HEAD_SIZE // 2
    freq = jnp.exp(
        jnp.arange(half, dtype=jnp.int32).astype(jnp.float32) * (-2.0 * math.log(THETA) / HEAD_SIZE)
    )
    angle = freq[:, None] * positions.astype(jnp.float32)[None, :]
    return jnp.cos(angle), jnp.sin(angle)


def dot_nn(left, right):
    return jnp.dot(left, right, preferred_element_type=jnp.float32)


def dot_nt(left, right):
    return lax.dot_general(
        left, right, (((1,), (1,)), ((), ())), preferred_element_type=jnp.float32
    )


def dot_tn(left, right):
    return lax.dot_general(
        left, right, (((0,), (0,)), ((), ())), preferred_element_type=jnp.float32
    )


def dot_any(left, right, left_dim, right_dim):
    return lax.dot_general(
        left, right, (((left_dim,), (right_dim,)), ((), ())), preferred_element_type=jnp.float32
    )


def turned(values, cosine, sine):
    half = HEAD_SIZE // 2
    out = []
    for head in range(values.shape[0] // HEAD_SIZE):
        first = values[head * HEAD_SIZE : head * HEAD_SIZE + half]
        second = values[head * HEAD_SIZE + half : (head + 1) * HEAD_SIZE]
        out.append(first * cosine - second * sine)
        out.append(second * cosine + first * sine)
    return jnp.concatenate(out, axis=0)


def by_position(values):
    block = values.shape[1] // 4
    place = [BLOCK_ORDER.index(i) for i in range(4)]
    return jnp.concatenate([values[:, p * block : (p + 1) * block] for p in place], axis=1)


def by_block(values):
    block = values.shape[1] // 4
    return jnp.concatenate([values[:, p * block : (p + 1) * block] for p in BLOCK_ORDER], axis=1)


def queries_of(ref, group, part, block):
    start = group * GROUP_QUERIES * HEAD_SIZE
    heads = [
        ref[start + i * HEAD_SIZE : start + (i + 1) * HEAD_SIZE, part * block : (part + 1) * block]
        for i in range(GROUP_QUERIES)
    ]
    return jnp.concatenate(heads, axis=1)


def scores_of(keys, queries, block_index, block):
    scores = dot_any(keys, queries, 0, 0) * (1.0 / math.sqrt(HEAD_SIZE))
    key_place = lax.broadcasted_iota(jnp.int32, scores.shape, 0)
    lane = lax.broadcasted_iota(jnp.int32, scores.shape, 1)
    query_place = block_index * block + lax.rem(lane, block)
    return jnp.where(key_place <= query_place, scores, -1e30)


def front_kernel(
    me_ref, x_ref, own_ref, beside_ref, cross_ref, corner_ref, cos_ref, sin_ref,
    a1_ref, w_ref, gain_ref, q_ref, k_ref, v_ref, o_ref, lse_ref,
):
    me = me_ref[0]
    second = me_ref[1]
    width = x_ref.shape[0]
    block = x_ref.shape[1] // 4
    kv_width = k_ref.shape[0]
    q_rows = width // 4
    kv_rows = kv_width // 4
    for ref, k in ((own_ref, 0), (beside_ref, 1), (cross_ref, 3), (corner_ref, 2)):
        device = me ^ k
        w_ref[pl.ds(pl.multiple_of(device * q_rows, 16), q_rows), :] = ref[0:q_rows, :]
        for i in range(2):
            start = width + i * kv_width + device * kv_rows
            first = q_rows + i * kv_rows
            w_ref[pl.ds(pl.multiple_of(start, 16), kv_rows), :] = ref[first : first + kv_rows, :]
        gain_row = q_rows + 2 * kv_rows
        part_gains = ref[gain_row : gain_row + 8, 0:256].astype(jnp.float32).T
        gain_ref[pl.ds(pl.multiple_of(device * q_rows, 8), q_rows), :] = part_gains[0:q_rows, :]
    x = x_ref[...].astype(jnp.float32)
    scale = lax.rsqrt(jnp.mean(x * x, axis=0, keepdims=True) + EPS)
    a1_ref[...] = ((x * scale) * gain_ref[:, 0:1]).astype(jnp.bfloat16)
    start = pl.multiple_of(second * (2 * block), 2 * block)
    a1_own = a1_ref[:, pl.ds(start, 2 * block)]
    a1 = a1_ref[...]
    cos_own = cos_ref[:, pl.ds(start, 2 * block)]
    sin_own = sin_ref[:, pl.ds(start, 2 * block)]
    for group in range(KEY_VALUE_HEADS):
        q_start = group * GROUP_QUERIES * HEAD_SIZE
        q_stop = q_start + GROUP_QUERIES * HEAD_SIZE
        kv_start = group * HEAD_SIZE
        kv_stop = kv_start + HEAD_SIZE
        keys = dot_any(w_ref[width + kv_start : width + kv_stop, :], a1, 1, 0)
        keys = by_position(turned(keys, cos_ref[...], sin_ref[...])).astype(jnp.bfloat16)
        values = dot_any(w_ref[width + kv_width + kv_start : width + kv_width + kv_stop, :], a1, 1, 0)
        values = by_position(values).astype(jnp.bfloat16)
        k_ref[kv_start:kv_stop, :] = keys
        v_ref[kv_start:kv_stop, :] = values
        queries = dot_any(w_ref[q_start:q_stop, :], a1_own, 1, 0)
        q_ref[q_start:q_stop, :] = turned(queries, cos_own, sin_own).astype(jnp.bfloat16)
        for part in range(2):
            block_index = second if part == 0 else 3 - second
            used = 2 * block * (part + 1)
            scores = scores_of(keys[:, :used], queries_of(q_ref, group, part, block), block_index, block)
            peak = jnp.max(scores, axis=0, keepdims=True)
            probs = jnp.exp(scores - peak)
            total = jnp.sum(probs, axis=0, keepdims=True)
            mixed = dot_any(values[:, :used], probs.astype(jnp.bfloat16), 1, 0) / total
            logsum = peak + jnp.log(total)
            for i in range(GROUP_QUERIES):
                head = group * GROUP_QUERIES + i
                lanes = slice(i * block, (i + 1) * block)
                places = slice(part * block, (part + 1) * block)
                o_ref[head * HEAD_SIZE : (head + 1) * HEAD_SIZE, places] = mixed[:, lanes].astype(jnp.bfloat16)
                lse_ref[head : head + 1, places] = logsum[:, lanes]


def back_kernel(
    me_ref, do_ref, o_ref, q_ref, k_ref, v_ref, lse_ref, cos_ref, sin_ref, dq_ref, dkv_ref, sent_ref
):
    second = me_ref[1]
    block = q_ref.shape[1] // 2
    kv_width = k_ref.shape[0]
    start = pl.multiple_of(second * (2 * block), 2 * block)
    cos_own = cos_ref[:, pl.ds(start, 2 * block)]
    sin_own = sin_ref[:, pl.ds(start, 2 * block)]
    scale = 1.0 / math.sqrt(HEAD_SIZE)
    for group in range(KEY_VALUE_HEADS):
        kv_start = group * HEAD_SIZE
        kv_stop = kv_start + HEAD_SIZE
        d_keys = d_values = None
        for part in (1, 0):
            block_index = second if part == 0 else 3 - second
            used = 2 * block * (part + 1)
            keys = k_ref[kv_start:kv_stop, :used]
            values = v_ref[kv_start:kv_stop, :used]
            queries = queries_of(q_ref, group, part, block)
            grads = queries_of(do_ref, group, part, block)
            outs = queries_of(o_ref, group, part, block)
            heads = range(group * GROUP_QUERIES, (group + 1) * GROUP_QUERIES)
            logsum = jnp.concatenate(
                [lse_ref[h : h + 1, part * block : (part + 1) * block] for h in heads], axis=1
            )
            probs = jnp.exp(scores_of(keys, queries, block_index, block) - logsum)
            delta = jnp.sum(grads.astype(jnp.float32) * outs.astype(jnp.float32), axis=0, keepdims=True)
            d_probs = dot_any(values, grads, 0, 0)
            d_scores = (probs * (d_probs - delta) * scale).astype(jnp.bfloat16)
            d_queries = dot_any(keys, d_scores, 1, 0)
            for i, h in enumerate(heads):
                places = slice(part * block, (part + 1) * block)
                back = turned(d_queries[:, i * block : (i + 1) * block], cos_own[:, places], -sin_own[:, places])
                dq_ref[h * HEAD_SIZE : (h + 1) * HEAD_SIZE, places] = back.astype(jnp.bfloat16)
            more_keys = dot_any(queries, d_scores, 1, 1)
            more_values = dot_any(grads, probs.astype(jnp.bfloat16), 1, 1)
            if part == 1:
                d_keys, d_values = more_keys, more_values
            else:
                d_keys = jnp.concatenate([d_keys[:, :used] + more_keys, d_keys[:, used:]], axis=1)
                d_values = jnp.concatenate([d_values[:, :used] + more_values, d_values[:, used:]], axis=1)
        d_keys = turned(by_block(d_keys), cos_ref[...], -sin_ref[...])
        d_values = by_block(d_values)
        dkv_ref[kv_start:kv_stop, :] = d_keys
        dkv_ref[kv_width + kv_start : kv_width + kv_stop, :] = d_values
        sent_ref[kv_start:kv_stop, :] = d_keys.astype(jnp.bfloat16)
        sent_ref[kv_width + kv_start : kv_width + kv_stop, :] = d_values.astype(jnp.bfloat16)


def whole(kernel, outs, *args):
    vmem = pl.BlockSpec(memory_space=pltpu.VMEM)
    return pl.pallas_call(
        kernel,
        out_shape=outs,
        in_specs=[pl.BlockSpec(memory_space=pltpu.SMEM)] + [vmem] * (len(args) - 1),
        out_specs=[vmem] * len(outs),
        compiler_params=pltpu.CompilerParams(vmem_limit_bytes=40 * 1024 * 1024),
        cost_estimate=pl.CostEstimate(flops=1000000, transcendentals=0, bytes_accessed=1000000),
    )(*args)


class Order:
    def __init__(self):
        self.token = None

    def mark(self, value):
        self.token = value

    def hold(self, *values):
        if self.token is None:
            return values if len(values) > 1 else values[0]
        held = lax.optimization_barrier(values + (self.token,))[:-1]
        return held if len(held) > 1 else held[0]


def rep_bits():
    count = lax.axis_size("rep")
    bits = count.bit_length() - 1
    assert 1 << bits == count and bits >= 3
    return bits


def row_major(values):
    return with_layout_constraint(values, Layout(major_to_minor=tuple(range(values.ndim))))


def swap_over_rep(held, bit, axis):
    count = lax.axis_size("rep")
    mine = (lax.axis_index("rep") >> bit) & 1
    away = lax.dynamic_index_in_dim(held, 1 - mine, axis, keepdims=False).astype(jnp.bfloat16)
    came = lax.ppermute(away, "rep", [(i, i ^ (1 << bit)) for i in range(count)])
    return lax.dynamic_index_in_dim(held, mine, axis, keepdims=False), came, away


def joined(pair):
    return pair[0] + pair[1].astype(jnp.float32)


def halve_lanes_over_rep(held, bit):
    count = lax.axis_size("rep")
    upper = ((lax.axis_index("rep") >> bit) & 1) == 1
    half = held.shape[1] // 2
    away = jnp.where(upper, held[:, :half], held[:, half:]).astype(jnp.bfloat16)
    came = lax.ppermute(away, "rep", [(i, i ^ (1 << bit)) for i in range(count)])
    return jnp.where(upper, held[:, half:], held[:, :half]), came, away


class RepSum:
    def __init__(self, partial, order):
        bits = rep_bits()
        self.bits_to_go = list(order) + list(range(len(order), bits))
        self.left = list(range(bits))
        self.held = partial.reshape((2,) * bits + partial.shape[1:])
        self.step()

    def step(self):
        bit = self.bits_to_go.pop(0)
        axis = len(self.left) - 1 - self.left.index(bit)
        self.left.remove(bit)
        self.kept, self.came, self.sent = swap_over_rep(self.held, bit, axis)

    def next(self, order):
        self.held = joined((self.kept, order.hold(self.came)))
        self.step()
        order.mark(self.sent)

    def end(self, order):
        while self.bits_to_go:
            self.next(order)
        return joined((self.kept, order.hold(self.came)))


def by_rep(partial):
    count = lax.axis_size("rep")
    return partial.reshape((count, partial.shape[0] // count) + partial.shape[1:])


def per_device(
    block_input,
    cotangent,
    norm_gains,
    w_query,
    key_weight,
    value_weight,
    w_out,
    w_gate,
    w_up,
    w_down,
):
    bf16 = jnp.bfloat16
    me = lax.axis_index("grp")
    rows = block_input.shape[1]
    width = block_input.shape[2]
    half_rows = 2 * rows
    kv_width = KEY_VALUE_HEADS * HEAD_SIZE
    slice_width = w_query.shape[1]
    kv_slice = key_weight.shape[1]
    hidden_slice = w_gate.shape[1]
    scale = 1.0 / math.sqrt(HEAD_SIZE)
    second_set = (me == 1) | (me == 2)
    own_start = second_set.astype(jnp.int32) * half_rows
    beside_start = half_rows - own_start
    own_block_start = jnp.where(me < 2, 0, rows)

    def own_half(values):
        return lax.dynamic_slice_in_dim(values, own_start, half_rows, 0)

    def own_block(values):
        return lax.dynamic_slice_in_dim(values, own_block_start, rows, 0)

    def own_cols(values):
        return lax.dynamic_slice_in_dim(values, me * (values.shape[1] // 4), values.shape[1] // 4, 1)

    def in_pair(own, cross):
        return jnp.concatenate([jnp.where(me < 2, own, cross), jnp.where(me < 2, cross, own)], axis=0)

    def sets(own, beside):
        return jnp.where(second_set, beside, own), jnp.where(second_set, own, beside)

    def core_swap(values):
        return lax.ppermute(values, "grp", CORE_SWAP)

    def chip_cross(values):
        return lax.ppermute(values, "grp", CROSS_SWAP)

    def two_halves(own, beside):
        return jnp.concatenate(sets(own, beside), axis=0)

    def in_order(own, beside, cross, corner, order=(0, 1, 2, 3)):
        out = []
        for device in order:
            out.append(
                jnp.where(
                    me == device,
                    own,
                    jnp.where(me == device ^ 1, beside, jnp.where(me == device ^ 3, cross, corner)),
                )
            )
        return jnp.concatenate(out, axis=0)

    turn = Order()

    x_here = block_input[0]
    x_cross = chip_cross(x_here)
    qkv_sent = row_major(
        jnp.concatenate(
            [
                w_query.T,
                key_weight.T,
                value_weight.T,
                jnp.pad(norm_gains, ((0, 6), (0, width - slice_width))),
            ],
            axis=0,
        )
    )
    qkv_cross = chip_cross(qkv_sent)
    turn.mark(qkv_sent)
    qkv_beside = core_swap(turn.hold(qkv_sent))
    x_pair = in_pair(x_here, turn.hold(x_cross))
    x_all = two_halves(x_pair, core_swap(x_pair))
    turn.mark(x_pair)
    places = np.concatenate([np.arange(b * rows, (b + 1) * rows, dtype=np.int32) for b in BLOCK_ORDER])
    cosine, sine = rope_tables(turn.hold(jnp.asarray(places)))
    wo_sent = turn.hold(w_out).T
    dy_here, down_t = turn.hold(cotangent, w_down)
    dy_here = dy_here[0]
    down_t = down_t.T
    wo_beside = core_swap(wo_sent)
    dy_beside = core_swap(dy_here)

    def down_piece(k):
        return lax.dynamic_slice_in_dim(down_t, (me ^ k) * hidden_slice, hidden_slice, 1)

    down_own, down_near = down_piece(0), down_piece(1)
    down_far = jnp.concatenate([down_piece(3), down_piece(2)], axis=0)
    cosine, sine, wo_sent, down_own, down_near, down_far, x_all, dy_here = lax.optimization_barrier(
        (cosine, sine, wo_sent, down_own, down_near, down_far, x_all, dy_here)
    )
    turn.mark(down_far)
    qkv_cross = row_major(turn.hold(qkv_cross))
    qkv_corner = row_major(core_swap(qkv_cross))
    turn.mark(qkv_cross)
    wo_cross = chip_cross(turn.hold(wo_sent))
    dy_cross = chip_cross(turn.hold(dy_here))
    place = jnp.stack([me, second_set.astype(jnp.int32)])

    def shaped(*shape, kind=bf16):
        return jax.ShapeDtypeStruct(shape, kind)

    a1_t, weights, gains, q_t, k_t, v_t, o_t, logsum = whole(
        front_kernel,
        [
            shaped(width, 4 * rows),
            shaped(width + 2 * kv_width, width),
            shaped(width, 8, kind=jnp.float32),
            shaped(width, half_rows),
            shaped(kv_width, 4 * rows),
            shaped(kv_width, 4 * rows),
            shaped(width, half_rows),
            shaped(QUERY_HEADS + 1, half_rows, kind=jnp.float32),
        ],
        place, x_all.T, qkv_sent, qkv_beside, qkv_cross, qkv_corner, cosine, sine,
    )
    gain_attn = gains[:, 0]
    gain_ffn = gains[:, 1]
    xf = x_pair.astype(jnp.float32)
    turn.mark(o_t)
    down_cross = chip_cross(turn.hold(down_far))

    wo_cross, dy_cross = turn.hold(wo_cross, dy_cross)
    wo_t = in_order(wo_sent, wo_beside, wo_cross, core_swap(wo_cross))
    x2 = xf + dot_any(o_t, wo_t, 0, 1)
    r2 = norm_scale(x2)
    n2 = x2 * r2
    a2_own = (n2 * gain_ffn).astype(bf16)
    a2_beside = core_swap(a2_own)
    turn.mark(a2_own)
    down_cross = turn.hold(down_cross)
    down_core = core_swap(jnp.concatenate([down_near, down_cross[slice_width:]], axis=0))
    dy_all = in_order(dy_here, dy_beside, dy_cross, core_swap(dy_cross), BLOCK_ORDER)
    a2 = two_halves(a2_own, a2_beside)

    gate = dot_nn(a2, w_gate)
    up = dot_nn(a2, w_up)
    gate, up, dy_all = lax.optimization_barrier((gate, up, dy_all))
    turn.mark(up)
    o_beside = core_swap(turn.hold(o_t))
    sig = jax.nn.sigmoid(gate)
    act = gate * sig
    hidden = (act * up).astype(bf16)
    down_core = turn.hold(down_core)
    down_rows_t = in_order(
        down_own, down_core[:slice_width], down_cross[:slice_width], down_core[slice_width:]
    )
    d_hidden = dot_nn(dy_all, down_rows_t)
    d_gate = (d_hidden * up * sig * (1.0 + gate * (1.0 - sig))).astype(bf16)
    d_up = (d_hidden * act).astype(bf16)
    d_a2_part = (dot_nt(d_gate, w_gate) + dot_nt(d_up, w_up)).astype(bf16)

    beside_part = core_swap(lax.dynamic_slice_in_dim(d_a2_part, beside_start, half_rows, 0))
    chip_sum = own_half(d_a2_part).astype(jnp.float32) + beside_part.astype(jnp.float32)
    chip_sent = chip_sum.astype(bf16)
    other_chip = chip_cross(chip_sent)
    turn.mark(chip_sent)
    a2_late, d_gate, d_up, hidden = turn.hold(a2, d_gate, d_up, hidden)
    gate_sum = RepSum(by_rep(dot_tn(a2_late, d_gate)), (0, 1))
    turn.mark(gate_sum.sent)
    up_sum = RepSum(by_rep(dot_tn(turn.hold(a2_late), d_up)), (1, 0))
    turn.mark(up_sum.sent)
    g_down = dot_tn(turn.hold(dy_all), hidden).reshape(2, 2, slice_width, hidden_slice)
    down_pair = swap_over_rep(g_down, 0, 1)
    turn.mark(down_pair[2])

    out_part = dot_nt(turn.hold(hidden), down_rows_t).astype(bf16)
    out_beside = core_swap(lax.dynamic_slice_in_dim(out_part, beside_start, half_rows, 0))
    out_chip = own_half(out_part).astype(jnp.float32) + out_beside.astype(jnp.float32)
    out_away = lax.dynamic_slice_in_dim(out_chip, rows - own_block_start, rows, 0).astype(bf16)
    turn.mark(out_away)

    other_chip = turn.hold(other_chip)
    d_a2 = chip_sum + other_chip.astype(jnp.float32)
    dyf = own_half(dy_all).astype(jnp.float32)
    d_n2 = d_a2 * gain_ffn
    d_x2 = dyf + r2 * (d_n2 - n2 * jnp.mean(d_n2 * n2, axis=-1, keepdims=True))
    d_x2_low = d_x2.astype(bf16)

    def columns_of(own):
        away = lax.dynamic_slice_in_dim(own, (me ^ 1) * slice_width, slice_width, 1)
        return two_halves(own_cols(own), core_swap(away))

    d_o = row_major(dot_any(wo_t, d_x2_low, 0, 1).astype(bf16))
    turn.mark(d_o)
    out_cross = chip_cross(turn.hold(out_away))
    d_o = turn.hold(d_o)
    d_q, d_kv, d_kv_sent = whole(
        back_kernel,
        [
            shaped(width, half_rows),
            shaped(2 * kv_width, 4 * rows, kind=jnp.float32),
            shaped(2 * kv_width, 4 * rows),
        ],
        place, d_o, o_t, q_t, k_t, v_t, logsum, cosine, sine,
    )
    d_kv_beside = core_swap(d_kv_sent)
    d_q_away = lax.dynamic_slice_in_dim(d_q, (me ^ 1) * slice_width, slice_width, 0)
    d_q_kept = lax.dynamic_slice_in_dim(d_q, me * slice_width, slice_width, 0)
    d_q_halves = sets(d_q_kept, core_swap(d_q_away))
    turn.mark(d_q_away)
    gate_sum.next(turn)
    d_kv, d_kv_beside = turn.hold(d_kv, d_kv_beside)
    d_kv = (d_kv + d_kv_beside.astype(jnp.float32)).astype(bf16)

    def block_lanes(values):
        return jnp.where(me < 2, values[:, :rows], values[:, rows:])

    d_kv_half = jnp.where(second_set, d_kv[:, half_rows:], d_kv[:, :half_rows])
    d_block = lax.optimization_barrier(
        jnp.concatenate([block_lanes(d_q), block_lanes(d_kv_half)], axis=0)
    )
    d_a1 = dot_any(d_block, weights, 0, 0)
    x_block = x_here.astype(jnp.float32)
    r1_block = norm_scale(x_block)
    n1_block = x_block * r1_block
    g_attn = jnp.sum(d_a1 * n1_block, axis=0)
    g_ffn = jnp.sum(own_block(d_a2 * n2), axis=0)
    g_gains = jnp.stack([g_attn, g_ffn]).reshape(2, 4, slice_width).transpose(1, 0, 2)

    def gain_piece(k):
        return lax.dynamic_index_in_dim(g_gains, me ^ k, 0, keepdims=False)

    gains_came = (
        core_swap(gain_piece(1)),
        lax.ppermute(gain_piece(2), "grp", CHIP_SWAP),
        chip_cross(gain_piece(3)),
    )
    turn.mark(g_gains)

    kv_mine = [
        lax.dynamic_slice_in_dim(d_kv, i * kv_width + me * kv_slice, kv_slice, 0) for i in range(2)
    ]
    g_q = by_rep(dot_any(turn.hold(a1_t), jnp.concatenate(d_q_halves, axis=1), 1, 1))
    g_kv = by_rep(dot_any(turn.hold(a1_t), jnp.concatenate(kv_mine, axis=0), 1, 1))
    o_all = jnp.concatenate(sets(o_t, o_beside), axis=1)
    g_out = by_rep(dot_nn(turn.hold(o_all), columns_of(d_x2_low)))
    turn.mark(g_out)
    gains_came = turn.hold(*gains_came)
    g_gains = gain_piece(0) + gains_came[0] + gains_came[1] + gains_came[2]
    count = g_q.shape[0]
    share = g_q.shape[1]
    riders = jnp.broadcast_to(jnp.pad(g_gains, ((0, 6), (0, 0))), (count, 8, slice_width))

    def full_lanes(values):
        return jnp.pad(values, ((0, 0), (0, 0), (0, -values.shape[2] % 128)))

    bundle = jnp.concatenate([full_lanes(part) for part in (g_q, g_out, g_kv, riders)], axis=1)
    attn_sum = RepSum(row_major(bundle), (0, 1))
    turn.mark(attn_sum.sent)

    down_held = joined((down_pair[0], turn.hold(down_pair[1])))
    down_pair = swap_over_rep(down_held, 1, 0)
    turn.mark(down_pair[2])
    up_sum.next(turn)
    gate_sum.next(turn)

    d_a1_late, d_x2_late = turn.hold(d_a1, d_x2)
    d_n1 = d_a1_late * gain_attn
    input_grad = own_block(d_x2_late) + r1_block * (
        d_n1 - n1_block * jnp.mean(d_n1 * n1_block, axis=-1, keepdims=True)
    )
    block_output = own_block(x2) + own_block(out_chip) + turn.hold(out_cross).astype(jnp.float32)
    input_grad, block_output = lax.optimization_barrier((input_grad, block_output))
    turn.mark(block_output)

    attn_sum.next(turn)
    down_held = joined((down_pair[0], turn.hold(down_pair[1])))
    parts = count // 4
    down_pair = halve_lanes_over_rep(down_held, rep_bits() - 1)
    turn.mark(down_pair[2])
    up_sum.next(turn)
    attn_sum.next(turn)
    down_held = joined((down_pair[0], turn.hold(down_pair[1])))
    for bit in reversed(range(2, rep_bits() - 1)):
        down_held = joined(halve_lanes_over_rep(down_held, bit))
    homes = [
        (j * count + r, (r & 3) * count + j * parts + (r >> 2)) for r in range(count) for j in range(4)
    ]
    down_sent = down_held.astype(bf16)
    g_down = lax.ppermute(down_sent, ("grp", "rep"), homes)
    turn.mark(down_sent)
    g_gate = gate_sum.end(turn)
    g_up = up_sum.end(turn)
    g_down = turn.hold(g_down).astype(jnp.float32).T
    g_gate, g_up, g_down = lax.optimization_barrier((g_gate, g_up, g_down))
    turn.mark(g_down)
    g_attn_w = row_major(attn_sum.end(turn))
    g_kv = g_attn_w[2 * share : 3 * share]
    return (
        block_output[None],
        input_grad[None],
        g_attn_w[3 * share : 3 * share + 2, :slice_width],
        g_attn_w[:share, :slice_width],
        g_kv[:, :kv_slice],
        g_kv[:, kv_slice : 2 * kv_slice],
        g_attn_w[share : 2 * share, :slice_width],
        g_gate,
        g_up,
        g_down,
    )


def solution(mesh):
    rows = P("rep", "grp", None)
    weight = P(None, "grp")
    grad = P("rep", "grp")
    return jax.shard_map(
        per_device,
        mesh=mesh,
        in_specs=(rows, rows) + (weight,) * 8,
        out_specs=(rows, rows, weight) + (grad,) * 7,
        check_vma=False,
    )
```

```python
import math

import jax
import jax.numpy as jnp
import numpy as np
from jax import lax
from jax.experimental.layout import Layout, with_layout_constraint
from jax.experimental import pallas as pl
from jax.experimental.pallas import tpu as pltpu
from jax.sharding import PartitionSpec as P

HEAD_SIZE = 64
QUERY_HEADS = 15
KEY_VALUE_HEADS = 5
GROUP_QUERIES = QUERY_HEADS // KEY_VALUE_HEADS
EPS = 1e-05
THETA = 10000.0

BLOCK_ORDER = (0, 3, 1, 2)

CORE_SWAP = [(0, 1), (1, 0), (2, 3), (3, 2)]
CHIP_SWAP = [(0, 2), (2, 0), (1, 3), (3, 1)]
CROSS_SWAP = [(0, 3), (3, 0), (1, 2), (2, 1)]


def norm_scale(values):
    return lax.rsqrt(jnp.mean(values * values, axis=-1, keepdims=True) + EPS)


def rope_tables(positions):
    half = HEAD_SIZE // 2
    freq = jnp.exp(
        jnp.arange(half, dtype=jnp.int32).astype(jnp.float32) * (-2.0 * math.log(THETA) / HEAD_SIZE)
    )
    angle = freq[:, None] * positions.astype(jnp.float32)[None, :]
    return jnp.cos(angle), jnp.sin(angle)


def dot_nn(left, right):
    return jnp.dot(left, right, preferred_element_type=jnp.float32)


def dot_nt(left, right):
    return lax.dot_general(
        left, right, (((1,), (1,)), ((), ())), preferred_element_type=jnp.float32
    )


def dot_tn(left, right):
    return lax.dot_general(
        left, right, (((0,), (0,)), ((), ())), preferred_element_type=jnp.float32
    )


def dot_any(left, right, left_dim, right_dim):
    return lax.dot_general(
        left, right, (((left_dim,), (right_dim,)), ((), ())), preferred_element_type=jnp.float32
    )


def turned(values, cosine, sine):
    half = HEAD_SIZE // 2
    out = []
    for head in range(values.shape[0] // HEAD_SIZE):
        first = values[head * HEAD_SIZE : head * HEAD_SIZE + half]
        second = values[head * HEAD_SIZE + half : (head + 1) * HEAD_SIZE]
        out.append(first * cosine - second * sine)
        out.append(second * cosine + first * sine)
    return jnp.concatenate(out, axis=0)


def by_position(values):
    block = values.shape[1] // 4
    place = [BLOCK_ORDER.index(i) for i in range(4)]
    return jnp.concatenate([values[:, p * block : (p + 1) * block] for p in place], axis=1)


def by_block(values):
    block = values.shape[1] // 4
    return jnp.concatenate([values[:, p * block : (p + 1) * block] for p in BLOCK_ORDER], axis=1)


def queries_of(ref, group, part, block):
    start = group * GROUP_QUERIES * HEAD_SIZE
    heads = [
        ref[start + i * HEAD_SIZE : start + (i + 1) * HEAD_SIZE, part * block : (part + 1) * block]
        for i in range(GROUP_QUERIES)
    ]
    return jnp.concatenate(heads, axis=1)


def scores_of(keys, queries, block_index, block):
    scores = dot_any(keys, queries, 0, 0) * (1.0 / math.sqrt(HEAD_SIZE))
    key_place = lax.broadcasted_iota(jnp.int32, scores.shape, 0)
    lane = lax.broadcasted_iota(jnp.int32, scores.shape, 1)
    query_place = block_index * block + lax.rem(lane, block)
    return jnp.where(key_place <= query_place, scores, -1e30)


def front_kernel(
    me_ref, x_ref, own_ref, beside_ref, cross_ref, corner_ref, cos_ref, sin_ref,
    a1_ref, w_ref, gain_ref, q_ref, k_ref, v_ref, o_ref, lse_ref, gain_column,
):
    me = me_ref[0]
    second = me_ref[1]
    width = x_ref.shape[0]
    block = x_ref.shape[1] // 4
    kv_width = k_ref.shape[0]
    q_rows = width // 4
    kv_rows = kv_width // 4
    for ref, k in ((own_ref, 0), (beside_ref, 1), (cross_ref, 3), (corner_ref, 2)):
        device = me ^ k
        w_ref[pl.ds(pl.multiple_of(device * q_rows, 16), q_rows), :] = ref[0:q_rows, :]
        for i in range(2):
            start = width + i * kv_width + device * kv_rows
            first = q_rows + i * kv_rows
            w_ref[pl.ds(pl.multiple_of(start, 16), kv_rows), :] = ref[first : first + kv_rows, :]
        gain_row = q_rows + 2 * kv_rows
        part_gains = ref[gain_row : gain_row + 8, 0:256].astype(jnp.float32).T
        gain_column[pl.ds(pl.multiple_of(device * q_rows, 8), q_rows), :] = part_gains[0:q_rows, :]
    gain_ref[...] = gain_column[...].T
    x = x_ref[...].astype(jnp.float32)
    scale = lax.rsqrt(jnp.mean(x * x, axis=0, keepdims=True) + EPS)
    a1_ref[...] = ((x * scale) * gain_column[:, 0:1]).astype(jnp.bfloat16)
    start = pl.multiple_of(second * (2 * block), 2 * block)
    a1_own = a1_ref[:, pl.ds(start, 2 * block)]
    a1 = a1_ref[...]
    cos_own = cos_ref[:, pl.ds(start, 2 * block)]
    sin_own = sin_ref[:, pl.ds(start, 2 * block)]
    for group in range(KEY_VALUE_HEADS):
        q_start = group * GROUP_QUERIES * HEAD_SIZE
        q_stop = q_start + GROUP_QUERIES * HEAD_SIZE
        kv_start = group * HEAD_SIZE
        kv_stop = kv_start + HEAD_SIZE
        keys = dot_any(w_ref[width + kv_start : width + kv_stop, :], a1, 1, 0)
        keys = by_position(turned(keys, cos_ref[...], sin_ref[...])).astype(jnp.bfloat16)
        values = dot_any(w_ref[width + kv_width + kv_start : width + kv_width + kv_stop, :], a1, 1, 0)
        values = by_position(values).astype(jnp.bfloat16)
        k_ref[kv_start:kv_stop, :] = keys
        v_ref[kv_start:kv_stop, :] = values
        queries = dot_any(w_ref[q_start:q_stop, :], a1_own, 1, 0)
        q_ref[q_start:q_stop, :] = turned(queries, cos_own, sin_own).astype(jnp.bfloat16)
        for part in range(2):
            block_index = second if part == 0 else 3 - second
            used = 2 * block * (part + 1)
            scores = scores_of(keys[:, :used], queries_of(q_ref, group, part, block), block_index, block)
            peak = jnp.max(scores, axis=0, keepdims=True)
            probs = jnp.exp(scores - peak)
            total = jnp.sum(probs, axis=0, keepdims=True)
            mixed = dot_any(values[:, :used], probs.astype(jnp.bfloat16), 1, 0) / total
            logsum = peak + jnp.log(total)
            for i in range(GROUP_QUERIES):
                head = group * GROUP_QUERIES + i
                lanes = slice(i * block, (i + 1) * block)
                places = slice(part * block, (part + 1) * block)
                o_ref[head * HEAD_SIZE : (head + 1) * HEAD_SIZE, places] = mixed[:, lanes].astype(jnp.bfloat16)
                lse_ref[head : head + 1, places] = logsum[:, lanes]


def back_kernel(
    me_ref, do_ref, o_ref, q_ref, k_ref, v_ref, lse_ref, cos_ref, sin_ref, dq_ref, dkv_ref, sent_ref
):
    second = me_ref[1]
    block = q_ref.shape[1] // 2
    kv_width = k_ref.shape[0]
    start = pl.multiple_of(second * (2 * block), 2 * block)
    cos_own = cos_ref[:, pl.ds(start, 2 * block)]
    sin_own = sin_ref[:, pl.ds(start, 2 * block)]
    scale = 1.0 / math.sqrt(HEAD_SIZE)
    for group in range(KEY_VALUE_HEADS):
        kv_start = group * HEAD_SIZE
        kv_stop = kv_start + HEAD_SIZE
        d_keys = d_values = None
        for part in (1, 0):
            block_index = second if part == 0 else 3 - second
            used = 2 * block * (part + 1)
            keys = k_ref[kv_start:kv_stop, :used]
            values = v_ref[kv_start:kv_stop, :used]
            queries = queries_of(q_ref, group, part, block)
            grads = queries_of(do_ref, group, part, block)
            outs = queries_of(o_ref, group, part, block)
            heads = range(group * GROUP_QUERIES, (group + 1) * GROUP_QUERIES)
            logsum = jnp.concatenate(
                [lse_ref[h : h + 1, part * block : (part + 1) * block] for h in heads], axis=1
            )
            probs = jnp.exp(scores_of(keys, queries, block_index, block) - logsum)
            delta = jnp.sum(grads.astype(jnp.float32) * outs.astype(jnp.float32), axis=0, keepdims=True)
            d_probs = dot_any(values, grads, 0, 0)
            d_scores = (probs * (d_probs - delta) * scale).astype(jnp.bfloat16)
            d_queries = dot_any(keys, d_scores, 1, 0)
            for i, h in enumerate(heads):
                places = slice(part * block, (part + 1) * block)
                back = turned(d_queries[:, i * block : (i + 1) * block], cos_own[:, places], -sin_own[:, places])
                dq_ref[h * HEAD_SIZE : (h + 1) * HEAD_SIZE, places] = back.astype(jnp.bfloat16)
            more_keys = dot_any(queries, d_scores, 1, 1)
            more_values = dot_any(grads, probs.astype(jnp.bfloat16), 1, 1)
            if part == 1:
                d_keys, d_values = more_keys, more_values
            else:
                d_keys = jnp.concatenate([d_keys[:, :used] + more_keys, d_keys[:, used:]], axis=1)
                d_values = jnp.concatenate([d_values[:, :used] + more_values, d_values[:, used:]], axis=1)
        d_keys = turned(by_block(d_keys), cos_ref[...], -sin_ref[...])
        d_values = by_block(d_values)
        dkv_ref[kv_start:kv_stop, :] = d_keys
        dkv_ref[kv_width + kv_start : kv_width + kv_stop, :] = d_values
        sent_ref[kv_start:kv_stop, :] = d_keys.astype(jnp.bfloat16)
        sent_ref[kv_width + kv_start : kv_width + kv_stop, :] = d_values.astype(jnp.bfloat16)


def whole(kernel, outs, *args, scratch=()):
    vmem = pl.BlockSpec(memory_space=pltpu.VMEM)
    return pl.pallas_call(
        kernel,
        out_shape=outs,
        in_specs=[pl.BlockSpec(memory_space=pltpu.SMEM)] + [vmem] * (len(args) - 1),
        out_specs=[vmem] * len(outs),
        scratch_shapes=scratch,
        compiler_params=pltpu.CompilerParams(vmem_limit_bytes=12 * 1024 * 1024),
        cost_estimate=pl.CostEstimate(flops=1000000, transcendentals=0, bytes_accessed=1000000),
    )(*args)


class Order:
    def __init__(self):
        self.token = None

    def mark(self, value):
        self.token = value

    def hold(self, *values):
        if self.token is None:
            return values if len(values) > 1 else values[0]
        held = lax.optimization_barrier(values + (self.token,))[:-1]
        return held if len(held) > 1 else held[0]


def rep_bits():
    count = lax.axis_size("rep")
    bits = count.bit_length() - 1
    assert 1 << bits == count and bits >= 3
    return bits


def row_major(values):
    return with_layout_constraint(values, Layout(major_to_minor=tuple(range(values.ndim))))


def swap_over_rep(held, bit, axis):
    count = lax.axis_size("rep")
    mine = (lax.axis_index("rep") >> bit) & 1
    away = lax.dynamic_index_in_dim(held, 1 - mine, axis, keepdims=False).astype(jnp.bfloat16)
    came = lax.ppermute(away, "rep", [(i, i ^ (1 << bit)) for i in range(count)])
    return lax.dynamic_index_in_dim(held, mine, axis, keepdims=False), came, away


def joined(pair):
    return pair[0] + pair[1].astype(jnp.float32)


def halve_lanes_over_rep(held, bit):
    count = lax.axis_size("rep")
    upper = ((lax.axis_index("rep") >> bit) & 1) == 1
    half = held.shape[1] // 2
    away = jnp.where(upper, held[:, :half], held[:, half:]).astype(jnp.bfloat16)
    came = lax.ppermute(away, "rep", [(i, i ^ (1 << bit)) for i in range(count)])
    return jnp.where(upper, held[:, half:], held[:, :half]), came, away


class RepSum:
    def __init__(self, partial, order):
        bits = rep_bits()
        self.bits_to_go = list(order) + list(range(len(order), bits))
        self.left = list(range(bits))
        self.held = partial.reshape((2,) * bits + partial.shape[1:])
        self.step()

    def step(self):
        bit = self.bits_to_go.pop(0)
        axis = len(self.left) - 1 - self.left.index(bit)
        self.left.remove(bit)
        self.kept, self.came, self.sent = swap_over_rep(self.held, bit, axis)

    def next(self, order):
        self.held = joined((self.kept, order.hold(self.came)))
        self.step()
        order.mark(self.sent)

    def end(self, order):
        while self.bits_to_go:
            self.next(order)
        return joined((self.kept, order.hold(self.came)))


def by_rep(partial):
    count = lax.axis_size("rep")
    return partial.reshape((count, partial.shape[0] // count) + partial.shape[1:])


def per_device(
    block_input,
    cotangent,
    norm_gains,
    w_query,
    key_weight,
    value_weight,
    w_out,
    w_gate,
    w_up,
    w_down,
):
    bf16 = jnp.bfloat16
    me = lax.axis_index("grp")
    rows = block_input.shape[1]
    width = block_input.shape[2]
    half_rows = 2 * rows
    kv_width = KEY_VALUE_HEADS * HEAD_SIZE
    slice_width = w_query.shape[1]
    kv_slice = key_weight.shape[1]
    hidden_slice = w_gate.shape[1]
    scale = 1.0 / math.sqrt(HEAD_SIZE)
    second_set = (me == 1) | (me == 2)
    own_start = second_set.astype(jnp.int32) * half_rows
    beside_start = half_rows - own_start
    own_block_start = jnp.where(me < 2, 0, rows)

    def own_half(values):
        return lax.dynamic_slice_in_dim(values, own_start, half_rows, 0)

    def own_block(values):
        return lax.dynamic_slice_in_dim(values, own_block_start, rows, 0)

    def own_cols(values):
        return lax.dynamic_slice_in_dim(values, me * (values.shape[1] // 4), values.shape[1] // 4, 1)

    def in_pair(own, cross):
        return jnp.concatenate([jnp.where(me < 2, own, cross), jnp.where(me < 2, cross, own)], axis=0)

    def sets(own, beside):
        return jnp.where(second_set, beside, own), jnp.where(second_set, own, beside)

    def core_swap(values):
        return lax.ppermute(values, "grp", CORE_SWAP)

    def chip_cross(values):
        return lax.ppermute(values, "grp", CROSS_SWAP)

    def two_halves(own, beside):
        return jnp.concatenate(sets(own, beside), axis=0)

    def in_order(own, beside, cross, corner, order=(0, 1, 2, 3)):
        out = []
        for device in order:
            out.append(
                jnp.where(
                    me == device,
                    own,
                    jnp.where(me == device ^ 1, beside, jnp.where(me == device ^ 3, cross, corner)),
                )
            )
        return jnp.concatenate(out, axis=0)

    turn = Order()

    x_here = block_input[0]
    x_cross = chip_cross(x_here)
    qkv_sent = row_major(
        jnp.concatenate(
            [
                w_query.T,
                key_weight.T,
                value_weight.T,
                jnp.pad(norm_gains, ((0, 6), (0, width - slice_width))),
            ],
            axis=0,
        )
    )
    qkv_cross = chip_cross(qkv_sent)
    turn.mark(qkv_sent)
    qkv_beside = core_swap(turn.hold(qkv_sent))
    x_pair = in_pair(x_here, turn.hold(x_cross))
    x_all = two_halves(x_pair, core_swap(x_pair))
    turn.mark(x_pair)
    places = np.concatenate([np.arange(b * rows, (b + 1) * rows, dtype=np.int32) for b in BLOCK_ORDER])
    cosine, sine = rope_tables(turn.hold(jnp.asarray(places)))
    wo_sent = turn.hold(w_out).T
    dy_here, down_t = turn.hold(cotangent, w_down)
    dy_here = dy_here[0]
    down_t = down_t.T
    wo_beside = core_swap(wo_sent)
    dy_beside = core_swap(dy_here)

    def down_piece(k):
        return lax.dynamic_slice_in_dim(down_t, (me ^ k) * hidden_slice, hidden_slice, 1)

    down_own, down_near = down_piece(0), down_piece(1)
    down_far = jnp.concatenate([down_piece(3), down_piece(2)], axis=0)
    cosine, sine, wo_sent, down_own, down_near, down_far, x_all, dy_here = lax.optimization_barrier(
        (cosine, sine, wo_sent, down_own, down_near, down_far, x_all, dy_here)
    )
    turn.mark(down_far)
    qkv_cross = row_major(turn.hold(qkv_cross))
    qkv_corner = row_major(core_swap(qkv_cross))
    turn.mark(qkv_cross)
    wo_cross = chip_cross(turn.hold(wo_sent))
    dy_cross = chip_cross(turn.hold(dy_here))
    place = jnp.stack([me, second_set.astype(jnp.int32)])

    def shaped(*shape, kind=bf16):
        return jax.ShapeDtypeStruct(shape, kind)

    a1_t, weights, gains, q_t, k_t, v_t, o_t, logsum = whole(
        front_kernel,
        [
            shaped(width, 4 * rows),
            shaped(width + 2 * kv_width, width),
            shaped(8, width, kind=jnp.float32),
            shaped(width, half_rows),
            shaped(kv_width, 4 * rows),
            shaped(kv_width, 4 * rows),
            shaped(width, half_rows),
            shaped(QUERY_HEADS + 1, half_rows, kind=jnp.float32),
        ],
        place, x_all.T, qkv_sent, qkv_beside, qkv_cross, qkv_corner, cosine, sine,
        scratch=[pltpu.VMEM((width, 8), jnp.float32)],
    )
    gain_attn = gains[0]
    gain_ffn = gains[1]
    xf = x_pair.astype(jnp.float32)
    turn.mark(o_t)
    down_cross = chip_cross(turn.hold(down_far))

    wo_cross, dy_cross = turn.hold(wo_cross, dy_cross)
    wo_t = in_order(wo_sent, wo_beside, wo_cross, core_swap(wo_cross))
    x2 = xf + dot_any(o_t, wo_t, 0, 1)
    r2 = norm_scale(x2)
    n2 = x2 * r2
    a2_own = (n2 * gain_ffn).astype(bf16)
    a2_beside = core_swap(a2_own)
    turn.mark(a2_own)
    down_cross = turn.hold(down_cross)
    down_core = core_swap(jnp.concatenate([down_near, down_cross[slice_width:]], axis=0))
    dy_all = in_order(dy_here, dy_beside, dy_cross, core_swap(dy_cross), BLOCK_ORDER)
    a2 = two_halves(a2_own, a2_beside)

    gate = dot_nn(a2, w_gate)
    up = dot_nn(a2, w_up)
    gate, up, dy_all = lax.optimization_barrier((gate, up, dy_all))
    turn.mark(up)
    o_beside = core_swap(turn.hold(o_t))
    sig = jax.nn.sigmoid(gate)
    act = gate * sig
    hidden = (act * up).astype(bf16)
    down_core = turn.hold(down_core)
    down_rows_t = in_order(
        down_own, down_core[:slice_width], down_cross[:slice_width], down_core[slice_width:]
    )
    d_hidden = dot_nn(dy_all, down_rows_t)
    d_gate = (d_hidden * up * sig * (1.0 + gate * (1.0 - sig))).astype(bf16)
    d_up = (d_hidden * act).astype(bf16)
    d_a2_part = (dot_nt(d_gate, w_gate) + dot_nt(d_up, w_up)).astype(bf16)

    beside_sent = lax.dynamic_slice_in_dim(d_a2_part, beside_start, half_rows, 0)
    beside_part = core_swap(beside_sent)
    turn.mark(beside_sent)
    a2_late, d_gate, d_up, hidden = turn.hold(a2, d_gate, d_up, hidden)
    g_gate = dot_tn(a2_late, d_gate)
    g_up = dot_tn(a2_late, d_up)
    g_down = dot_tn(dy_all, hidden)
    g_gate, g_up, g_down = lax.optimization_barrier((g_gate, g_up, g_down))
    turn.mark(g_gate)
    d_a2_kept, beside_part = turn.hold(d_a2_part, beside_part)
    chip_sum = own_half(d_a2_kept).astype(jnp.float32) + beside_part.astype(jnp.float32)
    chip_sent = chip_sum.astype(bf16)
    other_chip = chip_cross(chip_sent)
    turn.mark(chip_sent)
    g_gate, g_up, g_down = turn.hold(g_gate, g_up, g_down)
    gate_sum = RepSum(by_rep(g_gate), (0, 1))
    up_sum = RepSum(by_rep(g_up), (1, 0))
    down_pair = swap_over_rep(g_down.reshape(2, 2, slice_width, hidden_slice), 0, 1)
    turn.mark(down_pair[2])

    other_chip = turn.hold(other_chip)
    d_a2 = chip_sum + other_chip.astype(jnp.float32)
    dyf = own_half(dy_all).astype(jnp.float32)
    d_n2 = d_a2 * gain_ffn
    d_x2 = dyf + r2 * (d_n2 - n2 * jnp.mean(d_n2 * n2, axis=-1, keepdims=True))
    d_x2_low = d_x2.astype(bf16)

    def columns_of(own):
        away = lax.dynamic_slice_in_dim(own, (me ^ 1) * slice_width, slice_width, 1)
        return two_halves(own_cols(own), core_swap(away))

    d_o = row_major(dot_any(wo_t, d_x2_low, 0, 1).astype(bf16))
    turn.mark(d_o)
    d_o = turn.hold(d_o)
    d_q, d_kv, d_kv_sent = whole(
        back_kernel,
        [
            shaped(width, half_rows),
            shaped(2 * kv_width, 4 * rows, kind=jnp.float32),
            shaped(2 * kv_width, 4 * rows),
        ],
        place, d_o, o_t, q_t, k_t, v_t, logsum, cosine, sine,
    )
    d_kv_beside = core_swap(d_kv_sent)
    d_q_away = lax.dynamic_slice_in_dim(d_q, (me ^ 1) * slice_width, slice_width, 0)
    d_q_kept = lax.dynamic_slice_in_dim(d_q, me * slice_width, slice_width, 0)
    d_q_halves = sets(d_q_kept, core_swap(d_q_away))
    turn.mark(d_q_away)
    gate_sum.came, up_sum.came = turn.hold(gate_sum.came, up_sum.came)
    gate_sum.next(turn)
    up_sum.next(turn)

    def full_lanes(values):
        return jnp.pad(values, ((0, 0), (0, 0), (0, -values.shape[2] % 128)))

    o_all = jnp.concatenate(sets(*turn.hold(o_t, o_beside)), axis=1)
    out_sum = RepSum(row_major(full_lanes(by_rep(dot_nn(o_all, columns_of(d_x2_low))))), (0, 1))
    turn.mark(out_sum.sent)
    d_kv, d_kv_beside = turn.hold(d_kv, d_kv_beside)
    d_kv = (d_kv + d_kv_beside.astype(jnp.float32)).astype(bf16)

    d_kv_half = jnp.where(second_set, d_kv[:, half_rows:], d_kv[:, :half_rows])
    d_a1 = dot_any(jnp.concatenate([d_q, d_kv_half], axis=0), weights, 0, 0)
    x_block = x_here.astype(jnp.float32)
    r1_block = norm_scale(x_block)
    n1_block = x_block * r1_block
    g_attn = jnp.sum(d_a1 * (xf * norm_scale(xf)), axis=0)
    g_ffn = jnp.sum(d_a2 * n2, axis=0)
    g_gains = jnp.stack([g_attn, g_ffn]).reshape(2, 4, slice_width).transpose(1, 0, 2)

    def gain_piece(k):
        return lax.dynamic_index_in_dim(g_gains, me ^ k, 0, keepdims=False)

    gains_came = core_swap(gain_piece(1))
    turn.mark(g_gains)

    kv_mine = [
        lax.dynamic_slice_in_dim(d_kv, i * kv_width + me * kv_slice, kv_slice, 0) for i in range(2)
    ]
    g_q = by_rep(dot_any(turn.hold(a1_t), jnp.concatenate(d_q_halves, axis=1), 1, 1))
    g_kv = by_rep(dot_any(turn.hold(a1_t), jnp.concatenate(kv_mine, axis=0), 1, 1))
    turn.mark(g_q)
    gains_came, gate_sum.came = turn.hold(gains_came, gate_sum.came)
    g_gains = gain_piece(0) + gains_came
    count = g_q.shape[0]
    share = g_q.shape[1]
    riders = jnp.broadcast_to(jnp.pad(g_gains, ((0, 6), (0, 0))), (count, 8, slice_width))

    bundle = jnp.concatenate([full_lanes(part) for part in (g_q, g_kv, riders)], axis=1)
    attn_sum = RepSum(row_major(bundle), (0, 1))
    turn.mark(attn_sum.sent)

    out_part = dot_nt(turn.hold(hidden), down_rows_t).astype(bf16)
    out_beside = core_swap(lax.dynamic_slice_in_dim(out_part, beside_start, half_rows, 0))
    down_held = joined((down_pair[0], turn.hold(down_pair[1])))
    down_pair = swap_over_rep(down_held, 1, 0)
    turn.mark(down_pair[2])
    gate_sum.next(turn)
    up_sum.next(turn)
    out_sum.next(turn)
    out_chip = own_half(out_part).astype(jnp.float32) + turn.hold(out_beside).astype(jnp.float32)
    out_away = lax.dynamic_slice_in_dim(out_chip, rows - own_block_start, rows, 0).astype(bf16)
    out_cross = chip_cross(out_away)
    turn.mark(out_away)
    d_a1_late, d_x2_late = turn.hold(d_a1, d_x2)
    d_a1_late = own_block(d_a1_late)
    d_n1 = d_a1_late * gain_attn
    input_grad = own_block(d_x2_late) + r1_block * (
        d_n1 - n1_block * jnp.mean(d_n1 * n1_block, axis=-1, keepdims=True)
    )
    input_grad = lax.optimization_barrier(input_grad)
    turn.mark(input_grad)

    attn_sum.next(turn)
    down_held = joined((down_pair[0], turn.hold(down_pair[1])))
    parts = count // 4
    down_pair = halve_lanes_over_rep(down_held, rep_bits() - 1)
    turn.mark(down_pair[2])
    out_sum.next(turn)
    block_output = own_block(x2) + own_block(out_chip) + turn.hold(out_cross).astype(jnp.float32)
    block_output = lax.optimization_barrier(block_output)
    turn.mark(block_output)
    attn_sum.next(turn)
    down_held = joined((down_pair[0], turn.hold(down_pair[1])))
    for bit in reversed(range(2, rep_bits() - 1)):
        down_held = joined(halve_lanes_over_rep(down_held, bit))
    homes = [
        (j * count + r, (r & 3) * count + j * parts + (r >> 2)) for r in range(count) for j in range(4)
    ]
    down_sent = down_held.astype(bf16)
    g_down = lax.ppermute(down_sent, ("grp", "rep"), homes)
    turn.mark(down_sent)
    g_gate = gate_sum.end(turn)
    g_up = up_sum.end(turn)
    g_down = turn.hold(g_down).astype(jnp.float32).T
    g_gate, g_up, g_down = lax.optimization_barrier((g_gate, g_up, g_down))
    turn.mark(g_down)
    g_attn_w = row_major(attn_sum.end(turn))
    g_kv = g_attn_w[share : 2 * share]
    g_out = row_major(out_sum.end(turn))
    return (
        block_output[None],
        input_grad[None],
        g_attn_w[2 * share : 2 * share + 2, :slice_width],
        g_attn_w[:share, :slice_width],
        g_kv[:, :kv_slice],
        g_kv[:, kv_slice : 2 * kv_slice],
        g_out[:, :slice_width],
        g_gate,
        g_up,
        g_down,
    )


def solution(mesh):
    rows = P("rep", "grp", None)
    weight = P(None, "grp")
    grad = P("rep", "grp")
    return jax.shard_map(
        per_device,
        mesh=mesh,
        in_specs=(rows, rows) + (weight,) * 8,
        out_specs=(rows, rows, weight) + (grad,) * 7,
        check_vma=False,
    )
```

```python
import math

import jax
import jax.numpy as jnp
import numpy as np
from jax import lax
from jax.experimental.layout import Layout, with_layout_constraint
from jax.experimental import pallas as pl
from jax.experimental.pallas import tpu as pltpu
from jax.sharding import PartitionSpec as P

HEAD_SIZE = 64
QUERY_HEADS = 15
KEY_VALUE_HEADS = 5
GROUP_QUERIES = QUERY_HEADS // KEY_VALUE_HEADS
EPS = 1e-05
THETA = 10000.0

BLOCK_ORDER = (0, 3, 1, 2)

CORE_SWAP = [(0, 1), (1, 0), (2, 3), (3, 2)]
CHIP_SWAP = [(0, 2), (2, 0), (1, 3), (3, 1)]
CROSS_SWAP = [(0, 3), (3, 0), (1, 2), (2, 1)]


def norm_scale(values):
    return lax.rsqrt(jnp.mean(values * values, axis=-1, keepdims=True) + EPS)


def rope_tables(positions):
    half = HEAD_SIZE // 2
    freq = jnp.exp(
        jnp.arange(half, dtype=jnp.int32).astype(jnp.float32) * (-2.0 * math.log(THETA) / HEAD_SIZE)
    )
    angle = freq[:, None] * positions.astype(jnp.float32)[None, :]
    return jnp.cos(angle), jnp.sin(angle)


def dot_nn(left, right):
    return jnp.dot(left, right, preferred_element_type=jnp.float32)


def dot_nt(left, right):
    return lax.dot_general(
        left, right, (((1,), (1,)), ((), ())), preferred_element_type=jnp.float32
    )


def dot_tn(left, right):
    return lax.dot_general(
        left, right, (((0,), (0,)), ((), ())), preferred_element_type=jnp.float32
    )


def dot_any(left, right, left_dim, right_dim):
    return lax.dot_general(
        left, right, (((left_dim,), (right_dim,)), ((), ())), preferred_element_type=jnp.float32
    )


def turned(values, cosine, sine):
    half = HEAD_SIZE // 2
    out = []
    for head in range(values.shape[0] // HEAD_SIZE):
        first = values[head * HEAD_SIZE : head * HEAD_SIZE + half]
        second = values[head * HEAD_SIZE + half : (head + 1) * HEAD_SIZE]
        out.append(first * cosine - second * sine)
        out.append(second * cosine + first * sine)
    return jnp.concatenate(out, axis=0)


def by_position(values):
    block = values.shape[1] // 4
    place = [BLOCK_ORDER.index(i) for i in range(4)]
    return jnp.concatenate([values[:, p * block : (p + 1) * block] for p in place], axis=1)


def by_block(values):
    block = values.shape[1] // 4
    return jnp.concatenate([values[:, p * block : (p + 1) * block] for p in BLOCK_ORDER], axis=1)


def queries_of(ref, group, part, block):
    start = group * GROUP_QUERIES * HEAD_SIZE
    heads = [
        ref[start + i * HEAD_SIZE : start + (i + 1) * HEAD_SIZE, part * block : (part + 1) * block]
        for i in range(GROUP_QUERIES)
    ]
    return jnp.concatenate(heads, axis=1)


def scores_of(keys, queries, block_index, block):
    scores = dot_any(keys, queries, 0, 0) * (1.0 / math.sqrt(HEAD_SIZE))
    key_place = lax.broadcasted_iota(jnp.int32, scores.shape, 0)
    lane = lax.broadcasted_iota(jnp.int32, scores.shape, 1)
    query_place = block_index * block + lax.rem(lane, block)
    return jnp.where(key_place <= query_place, scores, -1e30)


def front_kernel(
    me_ref, x_ref, own_ref, beside_ref, cross_ref, corner_ref, cos_ref, sin_ref,
    a1_ref, w_ref, gain_ref, q_ref, k_ref, v_ref, o_ref, lse_ref, gain_column,
):
    me = me_ref[0]
    second = me_ref[1]
    width = x_ref.shape[0]
    block = x_ref.shape[1] // 4
    kv_width = k_ref.shape[0]
    q_rows = width // 4
    kv_rows = kv_width // 4
    for ref, k in ((own_ref, 0), (beside_ref, 1), (cross_ref, 3), (corner_ref, 2)):
        device = me ^ k
        w_ref[pl.ds(pl.multiple_of(device * q_rows, 16), q_rows), :] = ref[0:q_rows, :]
        for i in range(2):
            start = width + i * kv_width + device * kv_rows
            first = q_rows + i * kv_rows
            w_ref[pl.ds(pl.multiple_of(start, 16), kv_rows), :] = ref[first : first + kv_rows, :]
        gain_row = q_rows + 2 * kv_rows
        part_gains = ref[gain_row : gain_row + 8, 0:256].astype(jnp.float32).T
        gain_column[pl.ds(pl.multiple_of(device * q_rows, 8), q_rows), :] = part_gains[0:q_rows, :]
    gain_ref[...] = gain_column[...].T
    x = x_ref[...].astype(jnp.float32)
    scale = lax.rsqrt(jnp.mean(x * x, axis=0, keepdims=True) + EPS)
    a1_ref[...] = ((x * scale) * gain_column[:, 0:1]).astype(jnp.bfloat16)
    start = pl.multiple_of(second * (2 * block), 2 * block)
    a1_own = a1_ref[:, pl.ds(start, 2 * block)]
    a1 = a1_ref[...]
    cos_own = cos_ref[:, pl.ds(start, 2 * block)]
    sin_own = sin_ref[:, pl.ds(start, 2 * block)]
    for group in range(KEY_VALUE_HEADS):
        q_start = group * GROUP_QUERIES * HEAD_SIZE
        q_stop = q_start + GROUP_QUERIES * HEAD_SIZE
        kv_start = group * HEAD_SIZE
        kv_stop = kv_start + HEAD_SIZE
        keys = dot_any(w_ref[width + kv_start : width + kv_stop, :], a1, 1, 0)
        keys = by_position(turned(keys, cos_ref[...], sin_ref[...])).astype(jnp.bfloat16)
        values = dot_any(w_ref[width + kv_width + kv_start : width + kv_width + kv_stop, :], a1, 1, 0)
        values = by_position(values).astype(jnp.bfloat16)
        k_ref[kv_start:kv_stop, :] = keys
        v_ref[kv_start:kv_stop, :] = values
        queries = dot_any(w_ref[q_start:q_stop, :], a1_own, 1, 0)
        q_ref[q_start:q_stop, :] = turned(queries, cos_own, sin_own).astype(jnp.bfloat16)
        for part in range(2):
            block_index = second if part == 0 else 3 - second
            used = 2 * block * (part + 1)
            scores = scores_of(keys[:, :used], queries_of(q_ref, group, part, block), block_index, block)
            peak = jnp.max(scores, axis=0, keepdims=True)
            probs = jnp.exp(scores - peak)
            total = jnp.sum(probs, axis=0, keepdims=True)
            mixed = dot_any(values[:, :used], probs.astype(jnp.bfloat16), 1, 0) / total
            logsum = peak + jnp.log(total)
            for i in range(GROUP_QUERIES):
                head = group * GROUP_QUERIES + i
                lanes = slice(i * block, (i + 1) * block)
                places = slice(part * block, (part + 1) * block)
                o_ref[head * HEAD_SIZE : (head + 1) * HEAD_SIZE, places] = mixed[:, lanes].astype(jnp.bfloat16)
                lse_ref[head : head + 1, places] = logsum[:, lanes]


def back_kernel(
    me_ref, do_ref, o_ref, q_ref, k_ref, v_ref, lse_ref, cos_ref, sin_ref, dq_ref, dkv_ref, sent_ref
):
    second = me_ref[1]
    block = q_ref.shape[1] // 2
    kv_width = k_ref.shape[0]
    start = pl.multiple_of(second * (2 * block), 2 * block)
    cos_own = cos_ref[:, pl.ds(start, 2 * block)]
    sin_own = sin_ref[:, pl.ds(start, 2 * block)]
    scale = 1.0 / math.sqrt(HEAD_SIZE)
    for group in range(KEY_VALUE_HEADS):
        kv_start = group * HEAD_SIZE
        kv_stop = kv_start + HEAD_SIZE
        d_keys = d_values = None
        for part in (1, 0):
            block_index = second if part == 0 else 3 - second
            used = 2 * block * (part + 1)
            keys = k_ref[kv_start:kv_stop, :used]
            values = v_ref[kv_start:kv_stop, :used]
            queries = queries_of(q_ref, group, part, block)
            grads = queries_of(do_ref, group, part, block)
            outs = queries_of(o_ref, group, part, block)
            heads = range(group * GROUP_QUERIES, (group + 1) * GROUP_QUERIES)
            logsum = jnp.concatenate(
                [lse_ref[h : h + 1, part * block : (part + 1) * block] for h in heads], axis=1
            )
            probs = jnp.exp(scores_of(keys, queries, block_index, block) - logsum)
            delta = jnp.sum(grads.astype(jnp.float32) * outs.astype(jnp.float32), axis=0, keepdims=True)
            d_probs = dot_any(values, grads, 0, 0)
            d_scores = (probs * (d_probs - delta) * scale).astype(jnp.bfloat16)
            d_queries = dot_any(keys, d_scores, 1, 0)
            for i, h in enumerate(heads):
                places = slice(part * block, (part + 1) * block)
                back = turned(d_queries[:, i * block : (i + 1) * block], cos_own[:, places], -sin_own[:, places])
                dq_ref[h * HEAD_SIZE : (h + 1) * HEAD_SIZE, places] = back.astype(jnp.bfloat16)
            more_keys = dot_any(queries, d_scores, 1, 1)
            more_values = dot_any(grads, probs.astype(jnp.bfloat16), 1, 1)
            if part == 1:
                d_keys, d_values = more_keys, more_values
            else:
                d_keys = jnp.concatenate([d_keys[:, :used] + more_keys, d_keys[:, used:]], axis=1)
                d_values = jnp.concatenate([d_values[:, :used] + more_values, d_values[:, used:]], axis=1)
        d_keys = turned(by_block(d_keys), cos_ref[...], -sin_ref[...])
        d_values = by_block(d_values)
        dkv_ref[kv_start:kv_stop, :] = d_keys
        dkv_ref[kv_width + kv_start : kv_width + kv_stop, :] = d_values
        sent_ref[kv_start:kv_stop, :] = d_keys.astype(jnp.bfloat16)
        sent_ref[kv_width + kv_start : kv_width + kv_stop, :] = d_values.astype(jnp.bfloat16)


def whole(kernel, outs, *args, scratch=()):
    vmem = pl.BlockSpec(memory_space=pltpu.VMEM)
    return pl.pallas_call(
        kernel,
        out_shape=outs,
        in_specs=[pl.BlockSpec(memory_space=pltpu.SMEM)] + [vmem] * (len(args) - 1),
        out_specs=[vmem] * len(outs),
        scratch_shapes=scratch,
        compiler_params=pltpu.CompilerParams(vmem_limit_bytes=12 * 1024 * 1024),
        cost_estimate=pl.CostEstimate(flops=1000000, transcendentals=0, bytes_accessed=1000000),
    )(*args)


class Order:
    def __init__(self):
        self.token = None

    def mark(self, value):
        self.token = value

    def hold(self, *values):
        if self.token is None:
            return values if len(values) > 1 else values[0]
        held = lax.optimization_barrier(values + (self.token,))[:-1]
        return held if len(held) > 1 else held[0]


def rep_bits():
    count = lax.axis_size("rep")
    bits = count.bit_length() - 1
    assert 1 << bits == count and bits >= 3
    return bits


def row_major(values):
    return with_layout_constraint(values, Layout(major_to_minor=tuple(range(values.ndim))))


def swap_over_rep(held, bit, axis):
    count = lax.axis_size("rep")
    mine = (lax.axis_index("rep") >> bit) & 1
    away = lax.dynamic_index_in_dim(held, 1 - mine, axis, keepdims=False).astype(jnp.bfloat16)
    came = lax.ppermute(away, "rep", [(i, i ^ (1 << bit)) for i in range(count)])
    return lax.dynamic_index_in_dim(held, mine, axis, keepdims=False), came, away


def joined(pair):
    return pair[0] + pair[1].astype(jnp.float32)


def halve_lanes_over_rep(held, bit):
    count = lax.axis_size("rep")
    upper = ((lax.axis_index("rep") >> bit) & 1) == 1
    half = held.shape[1] // 2
    away = jnp.where(upper, held[:, :half], held[:, half:]).astype(jnp.bfloat16)
    came = lax.ppermute(away, "rep", [(i, i ^ (1 << bit)) for i in range(count)])
    return jnp.where(upper, held[:, half:], held[:, :half]), came, away


class RepSum:
    def __init__(self, partial, order):
        bits = rep_bits()
        self.bits_to_go = list(order) + list(range(len(order), bits))
        self.left = list(range(bits))
        self.held = partial.reshape((2,) * bits + partial.shape[1:])
        self.step()

    def step(self):
        bit = self.bits_to_go.pop(0)
        axis = len(self.left) - 1 - self.left.index(bit)
        self.left.remove(bit)
        self.kept, self.came, self.sent = swap_over_rep(self.held, bit, axis)

    def next(self, order):
        self.held = joined((self.kept, order.hold(self.came)))
        self.step()
        order.mark(self.sent)

    def end(self, order):
        while self.bits_to_go:
            self.next(order)
        return joined((self.kept, order.hold(self.came)))


def by_rep(partial):
    count = lax.axis_size("rep")
    return partial.reshape((count, partial.shape[0] // count) + partial.shape[1:])


def per_device(
    block_input,
    cotangent,
    norm_gains,
    w_query,
    key_weight,
    value_weight,
    w_out,
    w_gate,
    w_up,
    w_down,
):
    bf16 = jnp.bfloat16
    me = lax.axis_index("grp")
    rows = block_input.shape[1]
    width = block_input.shape[2]
    half_rows = 2 * rows
    kv_width = KEY_VALUE_HEADS * HEAD_SIZE
    slice_width = w_query.shape[1]
    kv_slice = key_weight.shape[1]
    hidden_slice = w_gate.shape[1]
    scale = 1.0 / math.sqrt(HEAD_SIZE)
    second_set = (me == 1) | (me == 2)
    own_start = second_set.astype(jnp.int32) * half_rows
    beside_start = half_rows - own_start
    own_block_start = jnp.where(me < 2, 0, rows)

    def own_half(values):
        return lax.dynamic_slice_in_dim(values, own_start, half_rows, 0)

    def own_block(values):
        return lax.dynamic_slice_in_dim(values, own_block_start, rows, 0)

    def own_cols(values):
        return lax.dynamic_slice_in_dim(values, me * (values.shape[1] // 4), values.shape[1] // 4, 1)

    def in_pair(own, cross):
        return jnp.concatenate([jnp.where(me < 2, own, cross), jnp.where(me < 2, cross, own)], axis=0)

    def sets(own, beside):
        return jnp.where(second_set, beside, own), jnp.where(second_set, own, beside)

    def core_swap(values):
        return lax.ppermute(values, "grp", CORE_SWAP)

    def chip_cross(values):
        return lax.ppermute(values, "grp", CROSS_SWAP)

    def two_halves(own, beside):
        return jnp.concatenate(sets(own, beside), axis=0)

    def in_order(own, beside, cross, corner, order=(0, 1, 2, 3)):
        out = []
        for device in order:
            out.append(
                jnp.where(
                    me == device,
                    own,
                    jnp.where(me == device ^ 1, beside, jnp.where(me == device ^ 3, cross, corner)),
                )
            )
        return jnp.concatenate(out, axis=0)

    turn = Order()

    x_here = block_input[0]
    x_cross = chip_cross(x_here)
    qkv_sent = row_major(
        jnp.concatenate(
            [
                w_query.T,
                key_weight.T,
                value_weight.T,
                jnp.pad(norm_gains, ((0, 6), (0, width - slice_width))),
            ],
            axis=0,
        )
    )
    qkv_cross = chip_cross(qkv_sent)
    turn.mark(qkv_sent)
    qkv_beside = core_swap(turn.hold(qkv_sent))
    x_pair = in_pair(x_here, turn.hold(x_cross))
    x_all = two_halves(x_pair, core_swap(x_pair))
    turn.mark(x_pair)
    places = np.concatenate([np.arange(b * rows, (b + 1) * rows, dtype=np.int32) for b in BLOCK_ORDER])
    cosine, sine = rope_tables(turn.hold(jnp.asarray(places)))
    wo_sent = turn.hold(w_out).T
    dy_here, down_t = turn.hold(cotangent, w_down)
    dy_here = dy_here[0]
    down_t = down_t.T
    wo_beside = core_swap(wo_sent)
    dy_beside = core_swap(dy_here)

    def down_piece(k):
        return lax.dynamic_slice_in_dim(down_t, (me ^ k) * hidden_slice, hidden_slice, 1)

    down_own, down_near = down_piece(0), down_piece(1)
    down_far = jnp.concatenate([down_piece(3), down_piece(2)], axis=0)
    cosine, sine, wo_sent, down_own, down_near, down_far, x_all, dy_here = lax.optimization_barrier(
        (cosine, sine, wo_sent, down_own, down_near, down_far, x_all, dy_here)
    )
    turn.mark(down_far)
    qkv_cross = row_major(turn.hold(qkv_cross))
    qkv_corner = row_major(core_swap(qkv_cross))
    turn.mark(qkv_cross)
    wo_cross = chip_cross(turn.hold(wo_sent))
    dy_cross = chip_cross(turn.hold(dy_here))
    place = jnp.stack([me, second_set.astype(jnp.int32)])

    def shaped(*shape, kind=bf16):
        return jax.ShapeDtypeStruct(shape, kind)

    a1_t, weights, gains, q_t, k_t, v_t, o_t, logsum = whole(
        front_kernel,
        [
            shaped(width, 4 * rows),
            shaped(width + 2 * kv_width, width),
            shaped(8, width, kind=jnp.float32),
            shaped(width, half_rows),
            shaped(kv_width, 4 * rows),
            shaped(kv_width, 4 * rows),
            shaped(width, half_rows),
            shaped(QUERY_HEADS + 1, half_rows, kind=jnp.float32),
        ],
        place, x_all.T, qkv_sent, qkv_beside, qkv_cross, qkv_corner, cosine, sine,
        scratch=[pltpu.VMEM((width, 8), jnp.float32)],
    )
    gain_attn = gains[0]
    gain_ffn = gains[1]
    xf = x_pair.astype(jnp.float32)
    turn.mark(o_t)
    down_cross = chip_cross(turn.hold(down_far))

    wo_cross, dy_cross = turn.hold(wo_cross, dy_cross)
    wo_t = in_order(wo_sent, wo_beside, wo_cross, core_swap(wo_cross))
    x2 = xf + dot_any(o_t, wo_t, 0, 1)
    r2 = norm_scale(x2)
    n2 = x2 * r2
    a2_own = (n2 * gain_ffn).astype(bf16)
    a2_beside = core_swap(a2_own)
    turn.mark(a2_own)
    down_cross = turn.hold(down_cross)
    down_core = core_swap(jnp.concatenate([down_near, down_cross[slice_width:]], axis=0))
    dy_all = in_order(dy_here, dy_beside, dy_cross, core_swap(dy_cross), BLOCK_ORDER)
    a2 = two_halves(a2_own, a2_beside)

    gate = dot_nn(a2, w_gate)
    up = dot_nn(a2, w_up)
    gate, up, dy_all = lax.optimization_barrier((gate, up, dy_all))
    turn.mark(up)
    o_beside = core_swap(turn.hold(o_t))
    sig = jax.nn.sigmoid(gate)
    act = gate * sig
    hidden = (act * up).astype(bf16)
    down_core = turn.hold(down_core)
    down_rows_t = in_order(
        down_own, down_core[:slice_width], down_cross[:slice_width], down_core[slice_width:]
    )
    d_hidden = dot_nn(dy_all, down_rows_t)
    d_gate = (d_hidden * up * sig * (1.0 + gate * (1.0 - sig))).astype(bf16)
    d_up = (d_hidden * act).astype(bf16)
    d_a2_part = (dot_nt(d_gate, w_gate) + dot_nt(d_up, w_up)).astype(bf16)

    beside_sent = lax.dynamic_slice_in_dim(d_a2_part, beside_start, half_rows, 0)
    beside_part = core_swap(beside_sent)
    turn.mark(beside_sent)
    a2_late, d_gate, d_up, hidden = turn.hold(a2, d_gate, d_up, hidden)
    g_gate = dot_tn(a2_late, d_gate)
    g_up = dot_tn(a2_late, d_up)
    g_down = dot_tn(dy_all, hidden)
    g_gate, g_up, g_down = lax.optimization_barrier((g_gate, g_up, g_down))
    turn.mark(g_gate)
    d_a2_kept, beside_part = turn.hold(d_a2_part, beside_part)
    chip_sum = own_half(d_a2_kept).astype(jnp.float32) + beside_part.astype(jnp.float32)
    chip_sent = chip_sum.astype(bf16)
    other_chip = chip_cross(chip_sent)
    turn.mark(chip_sent)
    g_gate, g_up, g_down = turn.hold(g_gate, g_up, g_down)
    gate_sum = RepSum(by_rep(g_gate), (0, 1))
    up_sum = RepSum(by_rep(g_up), (1, 0))
    down_pair = swap_over_rep(g_down.reshape(2, 2, slice_width, hidden_slice), 0, 1)
    turn.mark(down_pair[2])

    other_chip = turn.hold(other_chip)
    d_a2 = chip_sum + other_chip.astype(jnp.float32)
    dyf = own_half(dy_all).astype(jnp.float32)
    d_n2 = d_a2 * gain_ffn
    d_x2 = dyf + r2 * (d_n2 - n2 * jnp.mean(d_n2 * n2, axis=-1, keepdims=True))
    d_x2_low = d_x2.astype(bf16)

    def columns_of(own):
        away = lax.dynamic_slice_in_dim(own, (me ^ 1) * slice_width, slice_width, 1)
        return two_halves(own_cols(own), core_swap(away))

    d_o = row_major(dot_any(wo_t, d_x2_low, 0, 1).astype(bf16))
    turn.mark(d_o)
    d_o = turn.hold(d_o)
    d_q, d_kv, d_kv_sent = whole(
        back_kernel,
        [
            shaped(width, half_rows),
            shaped(2 * kv_width, 4 * rows, kind=jnp.float32),
            shaped(2 * kv_width, 4 * rows),
        ],
        place, d_o, o_t, q_t, k_t, v_t, logsum, cosine, sine,
    )
    d_kv_beside = core_swap(d_kv_sent)
    d_q_away = lax.dynamic_slice_in_dim(d_q, (me ^ 1) * slice_width, slice_width, 0)
    d_q_kept = lax.dynamic_slice_in_dim(d_q, me * slice_width, slice_width, 0)
    d_q_halves = sets(d_q_kept, core_swap(d_q_away))
    turn.mark(d_q_away)
    gate_sum.came, up_sum.came = turn.hold(gate_sum.came, up_sum.came)
    gate_sum.next(turn)
    up_sum.next(turn)

    def full_lanes(values):
        return jnp.pad(values, ((0, 0), (0, 0), (0, -values.shape[2] % 128)))

    d_kv, d_kv_beside = turn.hold(d_kv, d_kv_beside)
    d_kv = (d_kv + d_kv_beside.astype(jnp.float32)).astype(bf16)

    d_kv_half = jnp.where(second_set, d_kv[:, half_rows:], d_kv[:, :half_rows])
    d_a1 = dot_any(jnp.concatenate([d_q, d_kv_half], axis=0), weights, 0, 0)
    x_block = x_here.astype(jnp.float32)
    r1_block = norm_scale(x_block)
    n1_block = x_block * r1_block
    g_attn = jnp.sum(d_a1 * (xf * norm_scale(xf)), axis=0)
    g_ffn = jnp.sum(d_a2 * n2, axis=0)
    g_gains = jnp.stack([g_attn, g_ffn]).reshape(2, 4, slice_width).transpose(1, 0, 2)

    def gain_piece(k):
        return lax.dynamic_index_in_dim(g_gains, me ^ k, 0, keepdims=False)

    gains_came = core_swap(gain_piece(1))
    turn.mark(g_gains)

    kv_mine = [
        lax.dynamic_slice_in_dim(d_kv, i * kv_width + me * kv_slice, kv_slice, 0) for i in range(2)
    ]
    g_q = by_rep(dot_any(turn.hold(a1_t), jnp.concatenate(d_q_halves, axis=1), 1, 1))
    g_kv = by_rep(dot_any(turn.hold(a1_t), jnp.concatenate(kv_mine, axis=0), 1, 1))
    turn.mark(g_q)
    gains_came, gate_sum.came = turn.hold(gains_came, gate_sum.came)
    g_gains = gain_piece(0) + gains_came
    count = g_q.shape[0]
    share = g_q.shape[1]
    riders = jnp.broadcast_to(jnp.pad(g_gains, ((0, 6), (0, 0))), (count, 8, slice_width))

    bundle = jnp.concatenate([full_lanes(part) for part in (g_q, g_kv, riders)], axis=1)
    attn_sum = RepSum(row_major(bundle), (0, 1))
    turn.mark(attn_sum.sent)

    o_all = jnp.concatenate(sets(*turn.hold(o_t, o_beside)), axis=1)
    out_sum = RepSum(row_major(full_lanes(by_rep(dot_nn(o_all, columns_of(d_x2_low))))), (0, 1))
    turn.mark(out_sum.sent)
    out_part = dot_nt(turn.hold(hidden), down_rows_t).astype(bf16)
    out_beside = core_swap(lax.dynamic_slice_in_dim(out_part, beside_start, half_rows, 0))
    down_held = joined((down_pair[0], turn.hold(down_pair[1])))
    down_pair = swap_over_rep(down_held, 1, 0)
    turn.mark(down_pair[2])
    gate_sum.next(turn)
    up_sum.next(turn)
    out_sum.next(turn)
    out_chip = own_half(out_part).astype(jnp.float32) + turn.hold(out_beside).astype(jnp.float32)
    out_away = lax.dynamic_slice_in_dim(out_chip, rows - own_block_start, rows, 0).astype(bf16)
    out_cross = chip_cross(out_away)
    turn.mark(out_away)
    d_a1_late, d_x2_late = turn.hold(d_a1, d_x2)
    d_a1_late = own_block(d_a1_late)
    d_n1 = d_a1_late * gain_attn
    input_grad = own_block(d_x2_late) + r1_block * (
        d_n1 - n1_block * jnp.mean(d_n1 * n1_block, axis=-1, keepdims=True)
    )
    input_grad = lax.optimization_barrier(input_grad)
    turn.mark(input_grad)

    attn_sum.next(turn)
    down_held = joined((down_pair[0], turn.hold(down_pair[1])))
    parts = count // 4
    down_pair = halve_lanes_over_rep(down_held, rep_bits() - 1)
    turn.mark(down_pair[2])
    out_sum.next(turn)
    block_output = own_block(x2) + own_block(out_chip) + turn.hold(out_cross).astype(jnp.float32)
    block_output = lax.optimization_barrier(block_output)
    turn.mark(block_output)
    attn_sum.next(turn)
    down_held = joined((down_pair[0], turn.hold(down_pair[1])))
    for bit in reversed(range(2, rep_bits() - 1)):
        down_held = joined(halve_lanes_over_rep(down_held, bit))
    homes = [
        (j * count + r, (r & 3) * count + j * parts + (r >> 2)) for r in range(count) for j in range(4)
    ]
    down_sent = down_held.astype(bf16)
    g_down = lax.ppermute(down_sent, ("grp", "rep"), homes)
    turn.mark(down_sent)
    g_gate = gate_sum.end(turn)
    g_up = up_sum.end(turn)
    g_down = turn.hold(g_down).astype(jnp.float32).T
    g_gate, g_up, g_down = lax.optimization_barrier((g_gate, g_up, g_down))
    turn.mark(g_down)
    g_attn_w = row_major(attn_sum.end(turn))
    g_kv = g_attn_w[share : 2 * share]
    g_out = row_major(out_sum.end(turn))
    return (
        block_output[None],
        input_grad[None],
        g_attn_w[2 * share : 2 * share + 2, :slice_width],
        g_attn_w[:share, :slice_width],
        g_kv[:, :kv_slice],
        g_kv[:, kv_slice : 2 * kv_slice],
        g_out[:, :slice_width],
        g_gate,
        g_up,
        g_down,
    )


def solution(mesh):
    rows = P("rep", "grp", None)
    weight = P(None, "grp")
    grad = P("rep", "grp")
    return jax.shard_map(
        per_device,
        mesh=mesh,
        in_specs=(rows, rows) + (weight,) * 8,
        out_specs=(rows, rows, weight) + (grad,) * 7,
        check_vma=False,
    )
```
